768 devices in a mesh: gx: 16 (over x_hi, y), gy: 24 (over z, core), gz: 2 (over x_lo).
Axes of the slice: x: 4 (x_hi: 2, x_lo: 2; x = x_hi * 2 + x_lo), y: 8, z: 12, core: 2. Of those that a mesh axis runs over, the one named last changes fastest.
Arguments:
- u_now: float32 [3, 256, 384, 256], P(None, 'gx', 'gy', 'gz'), may hold values from -6 to 6
- u_prev: float32 [3, 256, 384, 256], P(None, 'gx', 'gy', 'gz'), may hold values from -6 to 6
- panels: bfloat16 [16, 2, 384, 48, 256], P('gx', 'gz', 'gy'), may hold values from -6 to 6
- panel_owner: int32 [16, 2, 384, 1], P('gx', 'gz'), may hold values from 0 to 23; in each aligned block of 16 rows (0 to 15, 16 to 31, ..., all dimensions but the last counted through in order) at most 2 rows name the same one
- panel_block: int32 [16, 2, 384], P('gx', 'gz'), may hold values from 0 to 2047
- coupling: float32 [3, 16, 16], replicated, may hold values from -1.5 to 1.5
- layer_depth: int32 [256], P('gz'), may hold values from 0 to 7, never falling along the last dimension, each value on 1 to 64 neighbouring positions
- layer_speed: float32 [8], replicated, may hold values from 0.04 to 0.3
- lateral: float32 [256, 384, 256], P('gx', 'gy', 'gz'), may hold values from 0.5 to 1
Outputs:
- u_final: float32 [3, 256, 384, 256], P(None, 'gx', 'gy', 'gz')
- u_before: float32 [3, 256, 384, 256], P(None, 'gx', 'gy', 'gz')
The draws below stay inside these ranges and needn't reach their ends.
Inputs may be any that keep to these rules, and one draw needn't show every extreme that they name: `panel_owner`: among the 16 panels of one device (an aligned block of rows) at most 2 have the same owner; in each draw some owner receives exactly 2 from some device. `layer_depth`: layers never decrease with depth; each layer spans 1 to 64 depths.
All inputs are finite; a program needn't handle non-finite values.
Results may differ from the reference program's by a relative error of at most 0.00038.
Values may be sent and summed in bfloat16 or wider, within the bound.
A program may use at most 64 MiB of HBM per device.

```python
import math
import jax
import jax.numpy as jnp
import numpy as np
from jax import lax

CX = 16
CY = 16
CZ = 128
PB = 16
NT = 256
PD = 16
NSTEP = 4
NL = 8
CAP = 2
NZB = 8
NBLK = 2048
NX = 256
NY = 384
NZ = 256
N_GX = 16
N_GY = 24
N_GZ = 2


def set_ends(values, key, smallest, top_value):
    spot = [jax.random.randint(jax.random.fold_in(key, axis), (), 0, length) for axis, length in enumerate(values.shape)]
    main_axis = values.shape.index(max(values.shape))
    next_to = spot[:main_axis] + [(spot[main_axis] + 1) % values.shape[main_axis]] + spot[main_axis + 1:]
    return values.at[tuple(spot)].set(smallest).at[tuple(next_to)].set(top_value)


def shard_levels(stream_key, extent, split, least, top_value):
    level, own = 1.0, jax.random.fold_in(stream_key, 6)
    for axis_at, shards_of in split:
        steps = jnp.exp(jax.random.uniform(jax.random.fold_in(own, axis_at), (shards_of,), jnp.float32, least / len(split), top_value / len(split)))
        level = level * jnp.repeat(steps, extent[axis_at] // shards_of).reshape([-1 if axis == axis_at else 1 for axis in range(len(extent))])
    return level


def profile(number_of, total, limit, slope):
    portions = [(1 << 20) // math.isqrt(standing ** slope) + 1 for standing in range(2, number_of + 1)]
    rest, given = total - limit - (number_of - 1), [1] * (number_of - 1)
    while rest > 0:
        movable = [i for i in range(number_of - 1) if given[i] < limit]
        whole, remaining = sum([portions[i] for i in movable]), rest
        for i in movable:
            more = min(limit - given[i], max(1, remaining * portions[i] // whole), rest)
            given[i] = given[i] + more
            rest = rest - more
    return np.array([limit] + given)


def uneven(own_key, number_of, total, limit, skew):
    if number_of == 2:
        one = jax.random.randint(own_key, (), max(1, total - limit), min(limit, total - 1) + 1)
        return jnp.stack([one, total - one])
    lengths = jnp.asarray(profile(number_of, total, limit, skew), jnp.int32)
    couples = (number_of - 1) // 2
    giver, receiver = lengths[1:1 + 2 * couples:2], lengths[2:2 + 2 * couples:2]
    margin = jnp.minimum(giver - 1, limit - receiver)
    shifted = jax.random.randint(jax.random.fold_in(own_key, 1), (couples,), 0, 1 << 20) % (margin + 1)
    lengths = lengths.at[1:1 + 2 * couples:2].set(giver - shifted).at[2:2 + 2 * couples:2].set(receiver + shifted)
    return lengths[jax.random.permutation(jax.random.fold_in(own_key, 2), number_of)]


def assign_block(key, own, number, rows, count, top, bound, lean):
    order = jax.random.permutation(key, count)
    packed, ordinary = load_shares(count, rows * top, bound, lean, True), load_shares(count, rows * top, bound, lean, False)
    places = jnp.arange(count)

    def named(lengths, turn):
        used = int((lengths > 0).sum())
        fixed = max(1, used // 4)
        shifted = fixed + (places - fixed + turn * (used - fixed)) % max(1, count - fixed)
        return jnp.zeros((count,), jnp.int32).at[order[jnp.where(places < fixed, places, shifted)]].set(jnp.asarray(lengths, jnp.int32))

    lengths = jnp.where(number % 4 == 0, named(packed, number // 4), named(ordinary, number - number // 4 - 1))
    mixed = jax.random.permutation(jax.random.fold_in(own, 3), count)
    giver, taker = mixed[0:count // 2 * 2:2], mixed[1:count // 2 * 2:2]
    margin = jnp.minimum(lengths[giver] - 1, bound - lengths[taker]) // 2
    margin = jnp.where((giver == order[0]) | (taker == order[0]) | (lengths[taker] == 0), 0, jnp.maximum(margin, 0))
    shifted = jax.random.randint(jax.random.fold_in(own, 4), (count // 2,), 0, 1 << 20) % (margin + 1)
    lengths = lengths.at[giver].add(-shifted).at[taker].add(shifted)
    labels = jnp.searchsorted(jnp.cumsum(lengths), jnp.arange(rows * top), side="right").astype(jnp.int32)
    table = labels.reshape(top, rows).T
    table = table[jax.random.permutation(jax.random.fold_in(own, 1), rows)]
    turn = jax.random.randint(jax.random.fold_in(own, 2), (rows, 1), 0, top)
    return jnp.take_along_axis(table, (jnp.arange(top)[None, :] + turn) % top, axis=1)


def load_shares(amount, total, reach, slope, full):
    loads = [(1 << 20) // math.isqrt(grade ** slope) + 1 for grade in range(1, amount + 1)]
    largest = reach if full else min(reach, max(-(-total // amount), total * loads[0] // sum(loads)))
    least = 1 if total - largest >= amount - 1 else 0
    counts, surplus = [largest] + [least] * (amount - 1), total - largest - least * (amount - 1)
    while surplus > 0:
        candidates = [i for i in range(1, amount) if counts[i] < largest] or [i for i in range(1, amount) if counts[i] < reach]
        pool, budget = sum([loads[i] for i in candidates]), surplus
        for i in candidates:
            more = min(reach - counts[i], max(1, budget * loads[i] // pool), surplus)
            counts[i] = counts[i] + more
            surplus = surplus - more
    return np.array(counts)


def centred(key, extent, spread, most, shards=(), kind=jnp.bfloat16):
    values = jax.random.normal(key, extent, jnp.float32) * spread
    if len(shards) > 0:
        values = shard_levels(key, extent, shards, -0.22, 0.18) * values
    return jnp.clip(values, min=-most, max=most).astype(kind)


def setup_inputs(seed: int = 0) -> dict:
    arg_keys = jax.random.split(jax.random.key(seed), 10)
    u_now = centred(arg_keys[0], (3, NX, NY, NZ), 1.0, 6.0, ((1, 16), (2, 24), (3, 2)), jnp.float32)
    u_prev = centred(arg_keys[1], (3, NX, NY, NZ), 1.0, 6.0, ((1, 16), (2, 24), (3, 2)), jnp.float32)
    panels = centred(arg_keys[2], (N_GX, N_GZ, N_GY * PD, 3 * PB, NT), 1.0, 6.0, ((0, 16), (1, 2), (2, 24)))
    panel_owner_keys = jax.random.split(jax.random.fold_in(arg_keys[3], 1), N_GX * N_GZ * (N_GY * PD) // PD)
    panel_owner_turns = jax.random.permutation(jax.random.fold_in(arg_keys[3], 3), N_GX * N_GZ * (N_GY * PD) // PD)
    panel_owner = jax.vmap(lambda own, number: assign_block(jax.random.fold_in(arg_keys[3], 2), own, number, PD, N_GY, 1, CAP, 2))(panel_owner_keys, panel_owner_turns).reshape((N_GX, N_GZ, N_GY * PD, 1))
    panel_block = set_ends(jax.random.randint(arg_keys[4], (N_GX, N_GZ, N_GY * PD), 0, NBLK), jax.random.fold_in(arg_keys[4], 1), 0, NBLK - 1).astype(jnp.int32)
    coupling = centred(arg_keys[5], (3, PB, PB), PB ** -0.5, 1.5, (), jnp.float32)
    layer_depth = jnp.searchsorted(jnp.cumsum(uneven(arg_keys[6], NL, NZ, NZ // 4, 0)), jnp.arange(NZ), side="right").astype(jnp.int32)
    layer_speed = jnp.clip(jnp.exp(jax.random.uniform(arg_keys[7], (NL,), jnp.float32, math.log(0.04), math.log(0.3))), 0.04, 0.3)
    lateral = jnp.clip(0.5 + 0.5 * jax.random.uniform(arg_keys[8], (NX, NY, NZ), jnp.float32) ** shard_levels(arg_keys[8], (NX, NY, NZ), ((0, 16), (1, 24), (2, 2)), -0.2, 0.2), 0.5, 1.0)
    return dict(u_now=u_now, u_prev=u_prev, panels=panels, panel_owner=panel_owner, panel_block=panel_block, coupling=coupling, layer_depth=layer_depth, layer_speed=layer_speed, lateral=lateral)


def wave_table():
    half = NT // 2
    freq = 2.0 * jnp.pi * (jnp.arange(half, dtype=jnp.float32) + 0.5) / NT
    times = 37.0 + jnp.arange(NSTEP, dtype=jnp.float32)
    phase = freq[:, None] * times[None, :]
    table = jnp.concatenate([jnp.cos(phase), jnp.sin(phase)], axis=0) / jnp.sqrt(jnp.float32(half))
    return table.astype(jnp.bfloat16)

def laplace(field):
    padded = jnp.pad(field, ((0, 0), (1, 1), (1, 1), (1, 1)))
    beside = padded[:, 2:, 1:-1, 1:-1] + padded[:, :-2, 1:-1, 1:-1]
    beside = beside + padded[:, 1:-1, 2:, 1:-1] + padded[:, 1:-1, :-2, 1:-1]
    beside = beside + padded[:, 1:-1, 1:-1, 2:] + padded[:, 1:-1, 1:-1, :-2]
    return beside - 6.0 * field

def reference(u_now, u_prev, panels, panel_owner, panel_block, coupling, layer_depth, layer_speed, lateral):
    table = wave_table()
    count = N_GX * N_GZ * N_GY * PD
    free = jnp.dot(panels.reshape(-1, NT), table, preferred_element_type=jnp.float32)
    free = free.reshape(count, 3, PB, NSTEP)
    force = jnp.einsum('cij,pcjn->pcin', coupling, free, precision=lax.Precision.HIGHEST)
    owner = panel_owner[..., 0]
    shape = owner.shape
    first = lax.broadcasted_iota(jnp.int32, shape, 0)
    depth = lax.broadcasted_iota(jnp.int32, shape, 1)
    xpos = (first * CX + panel_block // (CY * NZB)).reshape(-1).astype(jnp.int32)
    ypos = (owner * CY + panel_block // NZB % CY).reshape(-1).astype(jnp.int32)
    zbase = (depth * CZ + panel_block % NZB * PB).reshape(-1).astype(jnp.int32)
    zpos = zbase[:, None] + jnp.arange(PB, dtype=jnp.int32)[None, :]
    rate = lateral * layer_speed[layer_depth][None, None, :]
    for step in range(NSTEP):
        values = jnp.transpose(force[:, :, :, step], (1, 0, 2))
        drive = jnp.zeros((3, NX, NY, NZ), jnp.float32).at[:, xpos[:, None], ypos[:, None], zpos].add(values)
        u_next = 2.0 * u_now - u_prev + rate[None] * laplace(u_now) + drive
        u_prev = u_now
        u_now = u_next
    return (u_now, u_prev)
```

```python
import functools

import jax
import jax.numpy as jnp
import ml_dtypes
import numpy as np
from jax import lax
from jax.experimental import pallas as pl
from jax.experimental.pallas import tpu as pltpu
from jax.sharding import PartitionSpec as P

NSTEP = 4
MESH = pl.DeviceIdType.MESH
F32 = jnp.float32
BF16 = jnp.bfloat16


def wave_table(count):
    half = count // 2
    freq = np.float32(2.0 * np.pi) * (np.arange(half, dtype=np.float32) + np.float32(0.5)) / np.float32(count)
    times = np.float32(37.0) + np.arange(NSTEP, dtype=np.float32)
    phase = (freq[:, None] * times[None, :]).astype(np.float32)
    table = np.concatenate([np.cos(phase), np.sin(phase)], axis=0) / np.sqrt(np.float32(half))
    table = np.pad(table.T, ((0, 8 - NSTEP), (0, 0)))
    return table.astype(ml_dtypes.bfloat16)


def split_dot(a, b, dims):
    hi = b.astype(BF16)
    lo = (b - hi.astype(F32)).astype(BF16)
    one = a.astype(BF16)
    return lax.dot_general(one, hi, (dims, ((), ())), preferred_element_type=F32) + lax.dot_general(
        one, lo, (dims, ((), ())), preferred_element_type=F32
    )


def kernel(
    n_gx, n_gy, u_hbm, up_hbm, pan_hbm, own_hbm, blk_hbm, cpl_hbm, dep_hbm, spd_hbm, lat_hbm, tab_hbm,
    out_now, out_prev,
    U, up, pan, own, blk, cpl, dep, spd, lat, tab, G, W, D, msend, mrecv,
    ysend, yrecv, zsend, zrecv,
    in_sem, fsend_sem, frecv_sem, x_send, x_recv, y_send, y_recv, z_send, z_recv,
):
    gx, gy, gz = lax.axis_index("gx"), lax.axis_index("gy"), lax.axis_index("gz")
    loads = [
        pltpu.make_async_copy(pan_hbm, pan, in_sem.at[0]),
        pltpu.make_async_copy(tab_hbm, tab, in_sem.at[1]),
        pltpu.make_async_copy(own_hbm, own, in_sem.at[2]),
        pltpu.make_async_copy(blk_hbm, blk, in_sem.at[3]),
        pltpu.make_async_copy(cpl_hbm, cpl, in_sem.at[4]),
        pltpu.make_async_copy(u_hbm, U.at[0, :, 1:17], in_sem.at[5]),
        pltpu.make_async_copy(up_hbm, up, in_sem.at[6]),
        pltpu.make_async_copy(lat_hbm, lat, in_sem.at[7]),
        pltpu.make_async_copy(dep_hbm, dep, in_sem.at[8]),
        pltpu.make_async_copy(spd_hbm, spd, in_sem.at[9]),
    ]
    for copy in loads:
        copy.start()

    barrier = pltpu.get_barrier_semaphore()

    @pl.loop(1, n_gy)
    def _(k):
        pl.semaphore_signal(barrier, inc=1, device_id={"gy": lax.rem(gy + k, n_gy)}, device_id_type=MESH)

    pl.semaphore_signal(barrier, inc=1, device_id={"gz": 1 - gz}, device_id_type=MESH)
    has_left, has_right = gx > 0, gx < n_gx - 1
    has_down, has_up = gy > 0, gy < n_gy - 1

    @pl.when(has_left)
    def _():
        pl.semaphore_signal(barrier, inc=1, device_id={"gx": gx - 1}, device_id_type=MESH)

    @pl.when(has_right)
    def _():
        pl.semaphore_signal(barrier, inc=1, device_id={"gx": gx + 1}, device_id_type=MESH)

    @pl.when(jnp.logical_not(has_left))
    def _():
        U[:, :, 0] = jnp.zeros((NSTEP, 3, 16, 128), F32)

    @pl.when(jnp.logical_not(has_right))
    def _():
        U[:, :, 17] = jnp.zeros((NSTEP, 3, 16, 128), F32)

    @pl.when(jnp.logical_not(has_down))
    def _():
        yrecv[:, 0] = jnp.zeros((NSTEP, 3, 16, 128), F32)

    @pl.when(jnp.logical_not(has_up))
    def _():
        yrecv[:, 1] = jnp.zeros((NSTEP, 3, 16, 128), F32)

    edge = 127 - 127 * gz
    lane16 = lax.broadcasted_iota(jnp.int32, (16, 128), 1)
    row16 = lax.broadcasted_iota(jnp.int32, (16, 128), 0)

    for copy in loads[2:4]:
        copy.wait()
    owner = own[...]
    q = lax.broadcasted_iota(jnp.int32, (1, 384), 1)
    rank = jnp.zeros((1, 384), jnp.int32)
    for d in range(1, 16):
        same = jnp.logical_and(q % 16 >= d, pltpu.roll(owner, d, 1) == owner)
        rank = rank + same.astype(jnp.int32)
    own[...] = owner + 64 * rank
    code = own[...]
    k48 = lax.broadcasted_iota(jnp.int32, (48, 384), 0)
    q48 = lax.broadcasted_iota(jnp.int32, (48, 384), 1)
    slot, src = k48 // 24, k48 % 24
    mine = jnp.logical_and(code == gy + 64 * slot, q48 // 16 == src)
    slot_block = jnp.sum(jnp.where(mine, blk[...] + 1, 0), axis=1, keepdims=True) - 1

    tile = gy // 8
    off = (gy - 8 * tile) * 16
    lane1 = lax.broadcasted_iota(jnp.int32, (1, 128), 1)
    mycode = own[:, pl.ds(pl.multiple_of(tile * 128, 128), 128)]
    mycode = jnp.where(jnp.logical_and(lane1 >= off, lane1 < off + 16), mycode, 0)
    for s in (16, 32, 64):
        mycode = mycode + pltpu.roll(mycode, s, 1)
    r192 = lax.broadcasted_iota(jnp.int32, (192, 128), 0)
    l192 = lax.broadcasted_iota(jnp.int32, (192, 128), 1)
    want = (r192 % 24) + 64 * (r192 // 96)
    step_of = (r192 // 24) % 4
    pick = jnp.where(jnp.logical_and(mycode == want, l192 // 16 == step_of), 1.0, 0.0)

    for copy in loads[:2]:
        copy.wait()
    free = lax.dot_general(tab[...], pan[...], (((1,), (1,)), ((), ())), preferred_element_type=F32)
    G[...] = jnp.zeros_like(G)
    for p in range(16):
        G[:, p, :48] = free[:, 48 * p : 48 * p + 48]
    loads[4].wait()
    zero = jnp.zeros((16, 16), F32)
    stiff = jnp.concatenate(
        [jnp.concatenate([cpl[c] if c == k else zero for k in range(3)], axis=1) for c in range(3)], axis=0
    )
    force = lax.dot_general(
        G[...].reshape(128, 128)[:, :48], stiff, (((1,), (1,)), ((), ())),
        precision=lax.Precision.HIGHEST, preferred_element_type=F32,
    )
    picked = split_dot(pick, force, ((1,), (0,)))
    picked = jnp.concatenate([picked, jnp.zeros((192, 80), F32)], axis=1)
    lane24 = lax.broadcasted_iota(jnp.int32, (24, 128), 1)
    for c in range(3):
        message = jnp.zeros((24, 128), F32)
        for sn in range(8):
            part = picked[24 * sn : 24 * sn + 24]
            shift = (16 * (sn - c)) % 128
            if shift:
                part = pltpu.roll(part, shift, 1)
            message = jnp.where(lane24 // 16 == sn, part, message)
        msend[:, c, :] = message
    mrecv[gy] = msend[gy]

    near = 1 + has_left.astype(jnp.int32) + has_right.astype(jnp.int32)
    pl.semaphore_wait(barrier, n_gy - 1 + near)

    def message_copy(peer, sender):
        return pltpu.make_async_remote_copy(
            src_ref=msend.at[peer], dst_ref=mrecv.at[sender], send_sem=fsend_sem.at[peer],
            recv_sem=frecv_sem.at[sender], device_id={"gy": peer}, device_id_type=MESH,
        )

    @pl.loop(1, n_gy)
    def _(k):
        message_copy(lax.rem(gy + k, n_gy), gy).start()

    def x_copy(step, side):
        return pltpu.make_async_remote_copy(
            src_ref=U.at[step, :, 1 + 15 * side], dst_ref=U.at[step, :, 17 - 17 * side],
            send_sem=x_send.at[step, side], recv_sem=x_recv.at[step, side],
            device_id={"gx": gx - 1 + 2 * side}, device_id_type=MESH,
        )

    def y_copy(step, side):
        return pltpu.make_async_remote_copy(
            src_ref=ysend.at[step, side], dst_ref=yrecv.at[step, 1 - side],
            send_sem=y_send.at[step, side], recv_sem=y_recv.at[step, side],
            device_id={"gy": gy - 1 + 2 * side}, device_id_type=MESH,
        )

    def z_copy(step):
        return pltpu.make_async_remote_copy(
            src_ref=zsend.at[step], dst_ref=zrecv.at[step], send_sem=z_send.at[step], recv_sem=z_recv.at[step],
            device_id={"gz": 1 - gz}, device_id_type=MESH,
        )

    def start_faces(step):
        for side, there in ((0, has_left), (1, has_right)):
            pl.when(there)(lambda side=side: x_copy(step, side).start())
        for side, there in ((0, has_down), (1, has_up)):
            pl.when(there)(lambda side=side: y_copy(step, side).start())
        z_copy(step).start()

    def wait_faces(step):
        for side, there in ((0, has_right), (1, has_left)):
            pl.when(there)(lambda side=side: x_copy(step, side).wait_recv())
        for side, there in ((0, has_up), (1, has_down)):
            pl.when(there)(lambda side=side: y_copy(step, side).wait_recv())
        z_copy(step).wait_recv()

    def wait_sent(step):
        for side, there in ((0, has_left), (1, has_right)):
            pl.when(there)(lambda side=side: x_copy(step, side).wait_send())
        for side, there in ((0, has_down), (1, has_up)):
            pl.when(there)(lambda side=side: y_copy(step, side).wait_send())
        z_copy(step).wait_send()

    def pack(step, x, c, value, packed):
        ysend[step, 0, c, pl.ds(x, 1), :] = value[0:1]
        ysend[step, 1, c, pl.ds(x, 1), :] = value[15:16]
        place = 16 * c + x
        turned = pltpu.roll(value, lax.rem(place - edge + 128, 128), 1)
        return jnp.where(lane16 == place, turned, packed)

    loads[5].wait()

    def pack_first(x, packed):
        for c in range(3):
            packed = pack(0, x, c, U[0, c, x + 1], packed)
        return packed

    zsend[0] = lax.fori_loop(0, 16, pack_first, jnp.zeros((16, 128), F32))
    start_faces(0)

    for copy in loads[6:]:
        copy.wait()
    speed = jnp.zeros((1, 128), F32)
    for layer in range(spd.shape[1]):
        speed = jnp.where(dep[...] == layer, spd[0:1, layer : layer + 1], speed)
    lat[...] = lat[...] * speed[None]

    @pl.loop(1, n_gy)
    def _(k):
        peer = lax.rem(gy + n_gy - k, n_gy)
        message_copy(peer, peer).wait_recv()

    for s in range(2):
        block_s = slot_block[24 * s : 24 * s + 24]
        zb = jnp.bitwise_and(block_s, 7)
        for c in range(3):
            row = mrecv[:, c, :]
            for b in range(3):
                row = jnp.where(jnp.bitwise_and(zb, 1 << b) > 0, pltpu.roll(row, 16 << b, 1), row)
            for n in range(NSTEP):
                shift = (-16 * (4 * s + n)) % 128
                moved = pltpu.roll(row, shift, 1) if shift else row
                at = (3 * n + c) * 128
                W[24 * s : 24 * s + 24, at : at + 128] = jnp.where(lane24 // 16 == zb, moved, 0.0)
    column = lax.shift_right_arithmetic(slot_block, 3)
    onehot = jnp.where(column == lax.broadcasted_iota(jnp.int32, (48, 256), 1), 1.0, 0.0)
    D[...] = split_dot(onehot, W[...], ((0,), (0,)))

    for step in range(NSTEP):
        wait_faces(step)
        halo_z = zrecv[step]

        def advance(x, packed, step=step):
            rate = lat[x]
            for c in range(3):
                v = U[step, c, x + 1]
                below = jnp.where(row16 == 0, yrecv[step, 0, c, pl.ds(x, 1), :], pltpu.roll(v, 1, 0))
                above = jnp.where(row16 == 15, yrecv[step, 1, c, pl.ds(x, 1), :], pltpu.roll(v, 15, 0))
                turned = pltpu.roll(halo_z, lax.rem(edge - (16 * c + x) + 128, 128), 1)
                halo = jnp.where(lane16 == edge, turned, 0.0)
                z0 = jnp.where(lane16 == 0, 0.0, pltpu.roll(v, 1, 1))
                z1 = jnp.where(lane16 == 127, 0.0, pltpu.roll(v, 127, 1))
                around = U[step, c, x] + U[step, c, x + 2] + below + above + (z0 + z1 + halo)
                old = up[c, x] if step == 0 else U[step - 1, c, x + 1]
                at = (3 * step + c) * 128
                drive = D[pl.ds(pl.multiple_of(16 * x, 16), 16), at : at + 128]
                new = (2.0 * v - old) + rate * (around - 6.0 * v) + drive
                if step < NSTEP - 1:
                    U[step + 1, c, x + 1] = new
                    packed = pack(step + 1, x, c, new, packed)
                else:
                    out_now[c, x] = new
                    out_prev[c, x] = v
            return packed

        packed = lax.fori_loop(0, 16, advance, jnp.zeros((16, 128), F32))
        if step < NSTEP - 1:
            zsend[step + 1] = packed
            start_faces(step + 1)

    for step in range(NSTEP):
        wait_sent(step)

    @pl.loop(1, n_gy)
    def _(k):
        message_copy(lax.rem(gy + k, n_gy), gy).wait_send()


def per_device(n_gx, n_gy, u_now, u_prev, panels, panel_owner, panel_block, coupling, layer_depth, layer_speed, lateral):
    spectral = panels.shape[4]
    count = panel_owner.shape[2]
    layers = layer_speed.shape[0]
    table = jnp.asarray(wave_table(spectral))
    anywhere = pl.BlockSpec(memory_space=pl.ANY)
    vmem = pl.BlockSpec(memory_space=pltpu.VMEM)
    dma = pltpu.SemaphoreType.DMA
    return pl.pallas_call(
        functools.partial(kernel, n_gx, n_gy),
        out_shape=(jax.ShapeDtypeStruct(u_now.shape, F32), jax.ShapeDtypeStruct(u_now.shape, F32)),
        in_specs=[anywhere] * 10,
        out_specs=(vmem, vmem),
        scratch_shapes=[
            pltpu.VMEM((NSTEP, 3, 18, 16, 128), F32),
            pltpu.VMEM(u_prev.shape, F32),
            pltpu.VMEM((768, spectral), BF16),
            pltpu.VMEM((1, count), jnp.int32),
            pltpu.VMEM((1, count), jnp.int32),
            pltpu.VMEM(coupling.shape, F32),
            pltpu.VMEM((1, 128), jnp.int32),
            pltpu.VMEM((1, layers), F32),
            pltpu.VMEM(lateral.shape, F32),
            pltpu.VMEM(table.shape, BF16),
            pltpu.VMEM((8, 16, 128), F32),
            pltpu.VMEM((48, 1536), F32),
            pltpu.VMEM((256, 1536), F32),
            pltpu.VMEM((24, 3, 128), F32),
            pltpu.VMEM((24, 3, 128), F32),
            pltpu.VMEM((NSTEP, 2, 3, 16, 128), F32),
            pltpu.VMEM((NSTEP, 2, 3, 16, 128), F32),
            pltpu.VMEM((NSTEP, 16, 128), F32),
            pltpu.VMEM((NSTEP, 16, 128), F32),
            dma((10,)),
            dma((24,)),
            dma((24,)),
            dma((NSTEP, 2)),
            dma((NSTEP, 2)),
            dma((NSTEP, 2)),
            dma((NSTEP, 2)),
            dma((NSTEP,)),
            dma((NSTEP,)),
        ],
        compiler_params=pltpu.CompilerParams(collective_id=0, has_side_effects=True),
        name="domain_reduction",
    )(
        u_now, u_prev, panels.reshape(768, spectral), panel_owner.reshape(1, count), panel_block.reshape(1, count),
        coupling, layer_depth.reshape(1, 128), layer_speed.reshape(1, layers), lateral, table,
    )


def solution(mesh):
    in_specs = (
        P(None, "gx", "gy", "gz"),
        P(None, "gx", "gy", "gz"),
        P("gx", "gz", "gy", None, None),
        P("gx", "gz", None, None),
        P("gx", "gz", None),
        P(),
        P("gz"),
        P(),
        P("gx", "gy", "gz"),
    )
    out_specs = (P(None, "gx", "gy", "gz"), P(None, "gx", "gy", "gz"))
    return jax.shard_map(
        functools.partial(per_device, mesh.shape["gx"], mesh.shape["gy"]),
        mesh=mesh, in_specs=in_specs, out_specs=out_specs, check_vma=False,
    )
```

```python
import functools

import jax
import jax.numpy as jnp
import ml_dtypes
import numpy as np
from jax import lax
from jax.experimental import pallas as pl
from jax.experimental.pallas import tpu as pltpu
from jax.sharding import PartitionSpec as P

NSTEP = 4
MESH = pl.DeviceIdType.MESH
F32 = jnp.float32
BF16 = jnp.bfloat16


def wave_table(count):
    half = count // 2
    freq = np.float32(2.0 * np.pi) * (np.arange(half, dtype=np.float32) + np.float32(0.5)) / np.float32(count)
    times = np.float32(37.0) + np.arange(NSTEP, dtype=np.float32)
    phase = (freq[:, None] * times[None, :]).astype(np.float32)
    table = np.concatenate([np.cos(phase), np.sin(phase)], axis=0) / np.sqrt(np.float32(half))
    table = np.pad(table.T, ((0, 8 - NSTEP), (0, 0)))
    return table.astype(ml_dtypes.bfloat16)


def two_parts(b):
    hi = b.astype(BF16)
    lo = (b - hi.astype(F32)).astype(BF16)
    return jnp.concatenate([hi, lo], axis=0)


def kernel(
    n_gx, n_gy, u_hbm, up_hbm, pan_hbm, own_hbm, blk_hbm, cpl_hbm, dep_hbm, spd_hbm, lat_hbm, tab_hbm,
    out_now, out_prev,
    U, up, pan, own, blk, cpl, dep, spd, lat, tab, G, D, msend, mrecv, zsend, zrecv,
    in_sem, fsend_sem, frecv_sem, x_send, x_recv, y_send, y_recv, z_send, z_recv,
):
    gx, gy, gz = lax.axis_index("gx"), lax.axis_index("gy"), lax.axis_index("gz")
    loads = [
        pltpu.make_async_copy(pan_hbm, pan, in_sem.at[0]),
        pltpu.make_async_copy(tab_hbm, tab, in_sem.at[1]),
        pltpu.make_async_copy(own_hbm, own, in_sem.at[2]),
        pltpu.make_async_copy(blk_hbm, blk, in_sem.at[3]),
        pltpu.make_async_copy(cpl_hbm, cpl, in_sem.at[4]),
        pltpu.make_async_copy(u_hbm, U.at[0, :, 1:17, 8:24], in_sem.at[5]),
        pltpu.make_async_copy(up_hbm, up, in_sem.at[6]),
        pltpu.make_async_copy(lat_hbm, lat, in_sem.at[7]),
        pltpu.make_async_copy(dep_hbm, dep, in_sem.at[8]),
        pltpu.make_async_copy(spd_hbm, spd, in_sem.at[9]),
    ]
    for at in (2, 0, 1, 3, 4, 5, 6, 7, 8, 9):
        loads[at].start()

    barrier = pltpu.get_barrier_semaphore()

    @pl.loop(1, n_gy)
    def _(k):
        pl.semaphore_signal(barrier, inc=1, device_id={"gy": lax.rem(gy + k, n_gy)}, device_id_type=MESH)

    pl.semaphore_signal(barrier, inc=1, device_id={"gz": 1 - gz}, device_id_type=MESH)
    has_left, has_right = gx > 0, gx < n_gx - 1
    has_down, has_up = gy > 0, gy < n_gy - 1

    @pl.when(has_left)
    def _():
        pl.semaphore_signal(barrier, inc=1, device_id={"gx": gx - 1}, device_id_type=MESH)

    @pl.when(has_right)
    def _():
        pl.semaphore_signal(barrier, inc=1, device_id={"gx": gx + 1}, device_id_type=MESH)

    @pl.when(jnp.logical_not(has_left))
    def _():
        U[:, :, 0, 8:24] = jnp.zeros((NSTEP, 3, 16, 128), F32)

    @pl.when(jnp.logical_not(has_right))
    def _():
        U[:, :, 17, 8:24] = jnp.zeros((NSTEP, 3, 16, 128), F32)

    @pl.when(jnp.logical_not(has_down))
    def _():
        U[:, :, 1:17, 0:8] = jnp.zeros((NSTEP, 3, 16, 8, 128), F32)

    @pl.when(jnp.logical_not(has_up))
    def _():
        U[:, :, 1:17, 24:32] = jnp.zeros((NSTEP, 3, 16, 8, 128), F32)

    edge = 127 - 127 * gz
    lane16 = lax.broadcasted_iota(jnp.int32, (16, 128), 1)
    at_edge = lane16 == edge
    at_low, at_high = lane16 == 0, lane16 == 127

    loads[2].wait()
    owner = own[...]
    q = lax.broadcasted_iota(jnp.int32, (1, 384), 1)
    rank = jnp.zeros((1, 384), jnp.int32)
    for d in range(1, 16):
        same = jnp.logical_and(q % 16 >= d, pltpu.roll(owner, d, 1) == owner)
        rank = rank + same.astype(jnp.int32)
    own[...] = owner + 64 * rank

    tile = gy // 8
    off = (gy - 8 * tile) * 16
    lane1 = lax.broadcasted_iota(jnp.int32, (1, 128), 1)
    mycode = own[:, pl.ds(pl.multiple_of(tile * 128, 128), 128)]
    mycode = jnp.where(jnp.logical_and(lane1 >= off, lane1 < off + 16), mycode, 0)
    for s in (16, 32, 64):
        mycode = mycode + pltpu.roll(mycode, s, 1)
    r192 = lax.broadcasted_iota(jnp.int32, (192, 128), 0)
    l192 = lax.broadcasted_iota(jnp.int32, (192, 128), 1)
    want = (r192 % 24) + 64 * (r192 // 96)
    step_of = (r192 // 24) % 4
    pick = jnp.where(jnp.logical_and(mycode == want, l192 // 16 == step_of), 1.0, 0.0).astype(BF16)
    pick = jnp.concatenate([pick, pick], axis=1)

    G[...] = jnp.zeros_like(G)
    loads[4].wait()
    zero = jnp.zeros((16, 16), F32)
    stiff = jnp.concatenate(
        [jnp.concatenate([cpl[c] if c == k else zero for k in range(3)], axis=1) for c in range(3)], axis=0
    )
    loads[0].wait()
    loads[1].wait()
    free = lax.dot_general(tab[...], pan[...], (((1,), (1,)), ((), ())), preferred_element_type=F32)
    for p in range(16):
        G[:, p, :48] = free[:, 48 * p : 48 * p + 48]
    force = lax.dot_general(
        G[...].reshape(128, 128)[:, :48], stiff, (((1,), (1,)), ((), ())),
        precision=lax.Precision.HIGHEST, preferred_element_type=F32,
    )
    picked = jnp.dot(pick, two_parts(force), preferred_element_type=F32)
    picked = jnp.concatenate([picked, jnp.zeros((192, 80), F32)], axis=1)
    lane24 = lax.broadcasted_iota(jnp.int32, (24, 128), 1)
    for c in range(3):
        message = jnp.zeros((24, 128), F32)
        for sn in range(8):
            part = picked[24 * sn : 24 * sn + 24]
            shift = (16 * (sn - c)) % 128
            if shift:
                part = pltpu.roll(part, shift, 1)
            message = jnp.where(lane24 // 16 == sn, part, message)
        msend[:, c, :] = message
    mrecv[gy] = msend[gy]

    near = 1 + has_left.astype(jnp.int32) + has_right.astype(jnp.int32)
    loads[5].wait()
    pl.semaphore_wait(barrier, n_gy - 1 + near)

    def message_copy(peer, sender):
        return pltpu.make_async_remote_copy(
            src_ref=msend.at[peer], dst_ref=mrecv.at[sender], send_sem=fsend_sem.at[peer],
            recv_sem=frecv_sem.at[sender], device_id={"gy": peer}, device_id_type=MESH,
        )

    def x_copy(step, side):
        return pltpu.make_async_remote_copy(
            src_ref=U.at[step, :, 1 + 15 * side, 8:24], dst_ref=U.at[step, :, 17 - 17 * side, 8:24],
            send_sem=x_send.at[step, side], recv_sem=x_recv.at[step, side],
            device_id={"gx": gx - 1 + 2 * side}, device_id_type=MESH,
        )

    def y_copy(step, side):
        here, there = 8 + 15 * side, 24 - 17 * side
        return pltpu.make_async_remote_copy(
            src_ref=U.at[step, :, 1:17, here : here + 1], dst_ref=U.at[step, :, 1:17, there : there + 1],
            send_sem=y_send.at[step, side], recv_sem=y_recv.at[step, side],
            device_id={"gy": gy - 1 + 2 * side}, device_id_type=MESH,
        )

    def z_copy(step):
        return pltpu.make_async_remote_copy(
            src_ref=zsend.at[step], dst_ref=zrecv.at[step], send_sem=z_send.at[step], recv_sem=z_recv.at[step],
            device_id={"gz": 1 - gz}, device_id_type=MESH,
        )

    def start_x(step):
        for side, there in ((0, has_left), (1, has_right)):
            pl.when(there)(lambda side=side: x_copy(step, side).start())

    def start_yz(step):
        for side, there in ((0, has_down), (1, has_up)):
            pl.when(there)(lambda side=side: y_copy(step, side).start())
        z_copy(step).start()

    def wait_faces(step):
        for side, there in ((0, has_up), (1, has_down)):
            pl.when(there)(lambda side=side: y_copy(step, side).wait_recv())
        z_copy(step).wait_recv()
        for side, there in ((0, has_right), (1, has_left)):
            pl.when(there)(lambda side=side: x_copy(step, side).wait_recv())

    def wait_sent(step):
        for side, there in ((0, has_left), (1, has_right)):
            pl.when(there)(lambda side=side: x_copy(step, side).wait_send())
        for side, there in ((0, has_down), (1, has_up)):
            pl.when(there)(lambda side=side: y_copy(step, side).wait_send())
        z_copy(step).wait_send()

    def pack(place, value, packed):
        turned = pltpu.roll(value, place, 1) if place else value
        return jnp.where(lane16 == jnp.bitwise_and(edge + place, 127), turned, packed)

    start_x(0)

    @pl.loop(1, n_gy)
    def _(k):
        message_copy(lax.rem(gy + k, n_gy), gy).start()

    packed = jnp.zeros((16, 128), F32)
    for c in range(3):
        for x in range(16):
            packed = pack(16 * c + x, U[0, c, x + 1, 8:24], packed)
    zsend[0] = packed
    start_yz(0)

    loads[3].wait()
    k48 = lax.broadcasted_iota(jnp.int32, (48, 384), 0)
    q48 = lax.broadcasted_iota(jnp.int32, (48, 384), 1)
    late = k48 >= 32
    slot = jnp.where(late, (k48 - 32) // 8, k48 // 16)
    src = jnp.where(late, 16 + k48 % 8, k48 % 16)
    mine = jnp.logical_and(own[...] == gy + 64 * slot, q48 // 16 == src)
    slot_block = jnp.sum(jnp.where(mine, blk[...] + 1, 0), axis=1, keepdims=True) - 1
    column = lax.shift_right_arithmetic(slot_block, 3)
    hot = jnp.where(column == lax.broadcasted_iota(jnp.int32, (48, 256), 1), 1.0, 0.0)
    hot = jnp.transpose(jnp.concatenate([hot, jnp.zeros((80, 256), F32)], axis=0)).astype(BF16)
    hot_early = jnp.concatenate([hot[:, :32], hot[:, :32]], axis=1)
    hot_late = jnp.concatenate([hot[:, 32:48], hot[:, 32:48]], axis=1)

    for copy in loads[6:]:
        copy.wait()
    speed = jnp.zeros((1, 128), F32)
    for layer in range(spd.shape[1]):
        speed = jnp.where(dep[...] == layer, spd[0:1, layer : layer + 1], speed)
    lat[...] = lat[...] * speed[None]

    def turned_rows(first, count, at):
        out = []
        for s in range(2):
            zb = jnp.bitwise_and(slot_block[at + count * s : at + count * (s + 1)], 7)
            for c in range(3):
                row = mrecv[first : first + count, c, :]
                for b in range(3):
                    row = jnp.where(jnp.bitwise_and(zb, 1 << b) > 0, pltpu.roll(row, 16 << b, 1), row)
                out.append((s, c, zb, row))
        return out

    def placed(rows, count, hot, n):
        lanes = lax.broadcasted_iota(jnp.int32, (count, 128), 1) // 16
        parts = [[], []]
        for s, c, zb, row in rows:
            shift = (-16 * (4 * s + n)) % 128
            moved = pltpu.roll(row, shift, 1) if shift else row
            parts[s].append(jnp.where(lanes == zb, moved, 0.0))
        w = jnp.concatenate([jnp.concatenate(part, axis=1) for part in parts], axis=0)
        return jnp.dot(hot, two_parts(w), preferred_element_type=F32)

    def stencil(step, c, x, halo):
        v = U[step, c, x + 1, 8:24]
        place = 16 * c + x
        turned = pltpu.roll(halo, (128 - place) % 128, 1) if place else halo
        z = (
            jnp.where(at_low, 0.0, pltpu.roll(v, 1, 1))
            + jnp.where(at_high, 0.0, pltpu.roll(v, 127, 1))
            + jnp.where(at_edge, turned, 0.0)
        )
        y = U[step, c, x + 1, 7:23] + U[step, c, x + 1, 9:25]
        around = (U[step, c, x, 8:24] + U[step, c, x + 2, 8:24]) + y + z
        old = up[c, x] if step == 0 else U[step - 1, c, x + 1, 8:24]
        return (2.0 * v - old) + lat[x] * (around - 6.0 * v)

    order = [0, 15] + list(range(1, 15))

    def halo_of(step):
        return pltpu.roll(zrecv[step], jnp.bitwise_and(127 + 2 * gz, 127), 1)

    wait_faces(0)
    halo = halo_of(0)
    for x in order:
        for c in range(3):
            U[1, c, x + 1, 8:24] = stencil(0, c, x, halo)

    def message_wait(peer):
        pl.when(peer != gy)(lambda: message_copy(peer, peer).wait_recv())

    pl.loop(0, 16)(message_wait)
    rows = turned_rows(0, 16, 0)
    for n in range(NSTEP):
        D[n] = placed(rows, 16, hot_early, n)
    pl.loop(16, 24)(message_wait)
    rows = turned_rows(16, 8, 32)
    drive = D[0] + placed(rows, 8, hot_late, 0)
    packed = jnp.zeros((16, 128), F32)
    for x in order:
        for c in range(3):
            new = U[1, c, x + 1, 8:24] + drive[16 * x : 16 * x + 16, 128 * c : 128 * c + 128]
            U[1, c, x + 1, 8:24] = new
            packed = pack(16 * c + x, new, packed)
        if x == 15:
            start_x(1)
    zsend[1] = packed
    start_yz(1)
    for n in range(1, NSTEP):
        D[n] = D[n] + placed(rows, 8, hot_late, n)

    for step in range(1, NSTEP):
        wait_faces(step)
        halo = halo_of(step)
        packed = jnp.zeros((16, 128), F32)
        for x in order:
            for c in range(3):
                drive = D[step, 16 * x : 16 * x + 16, 128 * c : 128 * c + 128]
                new = stencil(step, c, x, halo) + drive
                if step < NSTEP - 1:
                    U[step + 1, c, x + 1, 8:24] = new
                    packed = pack(16 * c + x, new, packed)
                    if step == NSTEP - 2:
                        out_prev[c, x] = new
                else:
                    out_now[c, x] = new
            if step < NSTEP - 1 and x == 15:
                start_x(step + 1)
        if step < NSTEP - 1:
            zsend[step + 1] = packed
            start_yz(step + 1)

    for step in range(NSTEP):
        wait_sent(step)

    @pl.loop(1, n_gy)
    def _(k):
        message_copy(lax.rem(gy + k, n_gy), gy).wait_send()


def per_device(n_gx, n_gy, u_now, u_prev, panels, panel_owner, panel_block, coupling, layer_depth, layer_speed, lateral):
    spectral = panels.shape[4]
    count = panel_owner.shape[2]
    layers = layer_speed.shape[0]
    table = jnp.asarray(wave_table(spectral))
    anywhere = pl.BlockSpec(memory_space=pl.ANY)
    vmem = pl.BlockSpec(memory_space=pltpu.VMEM)
    dma = pltpu.SemaphoreType.DMA
    return pl.pallas_call(
        functools.partial(kernel, n_gx, n_gy),
        out_shape=(pltpu.VMEM(u_now.shape, F32), pltpu.VMEM(u_now.shape, F32)),
        in_specs=[anywhere] * 10,
        out_specs=(vmem, vmem),
        scratch_shapes=[
            pltpu.VMEM((NSTEP, 3, 18, 32, 128), F32),
            pltpu.VMEM(u_prev.shape, F32),
            pltpu.VMEM((768, spectral), BF16),
            pltpu.VMEM((1, count), jnp.int32),
            pltpu.VMEM((1, count), jnp.int32),
            pltpu.VMEM(coupling.shape, F32),
            pltpu.VMEM((1, 128), jnp.int32),
            pltpu.VMEM((1, layers), F32),
            pltpu.VMEM(lateral.shape, F32),
            pltpu.VMEM(table.shape, BF16),
            pltpu.VMEM((8, 16, 128), F32),
            pltpu.VMEM((NSTEP, 256, 384), F32),
            pltpu.VMEM((24, 3, 128), F32),
            pltpu.VMEM((24, 3, 128), F32),
            pltpu.VMEM((NSTEP, 16, 128), F32),
            pltpu.VMEM((NSTEP, 16, 128), F32),
            dma((10,)),
            dma((24,)),
            dma((24,)),
            dma((NSTEP, 2)),
            dma((NSTEP, 2)),
            dma((NSTEP, 2)),
            dma((NSTEP, 2)),
            dma((NSTEP,)),
            dma((NSTEP,)),
        ],
        compiler_params=pltpu.CompilerParams(collective_id=0, has_side_effects=True),
        name="domain_reduction",
    )(
        u_now, u_prev, panels.reshape(768, spectral), panel_owner.reshape(1, count), panel_block.reshape(1, count),
        coupling, layer_depth.reshape(1, 128), layer_speed.reshape(1, layers), lateral, table,
    )


def solution(mesh):
    in_specs = (
        P(None, "gx", "gy", "gz"),
        P(None, "gx", "gy", "gz"),
        P("gx", "gz", "gy", None, None),
        P("gx", "gz", None, None),
        P("gx", "gz", None),
        P(),
        P("gz"),
        P(),
        P("gx", "gy", "gz"),
    )
    out_specs = (P(None, "gx", "gy", "gz"), P(None, "gx", "gy", "gz"))
    return jax.shard_map(
        functools.partial(per_device, mesh.shape["gx"], mesh.shape["gy"]),
        mesh=mesh, in_specs=in_specs, out_specs=out_specs, check_vma=False,
    )
```

```python
import functools

import jax
import jax.numpy as jnp
import ml_dtypes
import numpy as np
from jax import lax
from jax.experimental import pallas as pl
from jax.experimental.pallas import tpu as pltpu
from jax.sharding import PartitionSpec as P

NSTEP = 4
MESH = pl.DeviceIdType.MESH
F32 = jnp.float32
BF16 = jnp.bfloat16


def wave_table(count):
    half = count // 2
    freq = np.float32(2.0 * np.pi) * (np.arange(half, dtype=np.float32) + np.float32(0.5)) / np.float32(count)
    times = np.float32(37.0) + np.arange(NSTEP, dtype=np.float32)
    phase = (freq[:, None] * times[None, :]).astype(np.float32)
    table = np.concatenate([np.cos(phase), np.sin(phase)], axis=0) / np.sqrt(np.float32(half))
    table = np.pad(table.T, ((0, 8 - NSTEP), (0, 0)))
    return table.astype(ml_dtypes.bfloat16)


def two_parts(b):
    hi = b.astype(BF16)
    lo = (b - hi.astype(F32)).astype(BF16)
    return jnp.concatenate([hi, lo], axis=0)


def kernel(
    n_gx, n_gy, u_hbm, up_hbm, pan_hbm, own_hbm, blk_hbm, cpl_hbm, dep_hbm, spd_hbm, lat_hbm, tab_hbm,
    out_now, out_prev,
    U, up, pan, own, blk, cpl, dep, spd, lat, tab, G, D, msend, mrecv, zsend, zrecv,
    in_sem, fsend_sem, frecv_sem, x_send, x_recv, y_send, y_recv, z_send, z_recv,
):
    gx, gy, gz = lax.axis_index("gx"), lax.axis_index("gy"), lax.axis_index("gz")
    loads = [
        pltpu.make_async_copy(pan_hbm, pan, in_sem.at[0]),
        pltpu.make_async_copy(tab_hbm, tab, in_sem.at[1]),
        pltpu.make_async_copy(own_hbm, own, in_sem.at[2]),
        pltpu.make_async_copy(blk_hbm, blk, in_sem.at[3]),
        pltpu.make_async_copy(cpl_hbm, cpl, in_sem.at[4]),
        pltpu.make_async_copy(u_hbm, U.at[0, :, 1:17, 8:24], in_sem.at[5]),
        pltpu.make_async_copy(up_hbm, up, in_sem.at[6]),
        pltpu.make_async_copy(lat_hbm, lat, in_sem.at[7]),
        pltpu.make_async_copy(dep_hbm, dep, in_sem.at[8]),
        pltpu.make_async_copy(spd_hbm, spd, in_sem.at[9]),
    ]
    for at in (2, 0, 1, 3, 4, 5, 6, 7, 8, 9):
        loads[at].start()

    barrier = pltpu.get_barrier_semaphore()

    has_left, has_right = gx > 0, gx < n_gx - 1
    has_down, has_up = gy > 0, gy < n_gy - 1

    pl.semaphore_signal(barrier, inc=1, device_id={"gz": 1 - gz}, device_id_type=MESH)

    @pl.when(has_down)
    def _():
        pl.semaphore_signal(barrier, inc=1, device_id={"gy": gy - 1}, device_id_type=MESH)

    @pl.when(has_left)
    def _():
        pl.semaphore_signal(barrier, inc=1, device_id={"gx": gx - 1}, device_id_type=MESH)

    @pl.when(has_right)
    def _():
        pl.semaphore_signal(barrier, inc=1, device_id={"gx": gx + 1}, device_id_type=MESH)

    @pl.loop(gy + 1, n_gy)
    def _(peer):
        pl.semaphore_signal(barrier, inc=1, device_id={"gy": peer}, device_id_type=MESH)

    @pl.when(jnp.logical_not(has_left))
    def _():
        U[:, :, 0, 8:24] = jnp.zeros((NSTEP, 3, 16, 128), F32)

    @pl.when(jnp.logical_not(has_right))
    def _():
        U[:, :, 17, 8:24] = jnp.zeros((NSTEP, 3, 16, 128), F32)

    @pl.when(jnp.logical_not(has_down))
    def _():
        U[:, :, 1:17, 0:8] = jnp.zeros((NSTEP, 3, 16, 8, 128), F32)

    @pl.when(jnp.logical_not(has_up))
    def _():
        U[:, :, 1:17, 24:32] = jnp.zeros((NSTEP, 3, 16, 8, 128), F32)

    edge = 127 - 127 * gz
    lane16 = lax.broadcasted_iota(jnp.int32, (16, 128), 1)
    at_edge = lane16 == edge
    at_low, at_high = lane16 == 0, lane16 == 127

    loads[2].wait()
    owner = own[...]
    q = lax.broadcasted_iota(jnp.int32, (1, 384), 1)
    rank = jnp.zeros((1, 384), jnp.int32)
    for d in range(1, 16):
        same = jnp.logical_and(q % 16 >= d, pltpu.roll(owner, d, 1) == owner)
        rank = rank + same.astype(jnp.int32)
    own[...] = owner + 64 * rank

    tile = gy // 8
    off = (gy - 8 * tile) * 16
    lane1 = lax.broadcasted_iota(jnp.int32, (1, 128), 1)
    mycode = own[:, pl.ds(pl.multiple_of(tile * 128, 128), 128)]
    mycode = jnp.where(jnp.logical_and(lane1 >= off, lane1 < off + 16), mycode, 0)
    for s in (16, 32, 64):
        mycode = mycode + pltpu.roll(mycode, s, 1)
    r192 = lax.broadcasted_iota(jnp.int32, (192, 128), 0)
    l192 = lax.broadcasted_iota(jnp.int32, (192, 128), 1)
    want = (r192 % 24) + 64 * (r192 // 96)
    step_of = (r192 // 24) % 4
    pick = jnp.where(jnp.logical_and(mycode == want, l192 // 16 == step_of), 1.0, 0.0).astype(BF16)
    pick = jnp.concatenate([pick, pick], axis=1)

    G[...] = jnp.zeros_like(G)
    loads[4].wait()
    zero = jnp.zeros((16, 16), F32)
    stiff = jnp.concatenate(
        [jnp.concatenate([cpl[c] if c == k else zero for k in range(3)], axis=1) for c in range(3)], axis=0
    )
    loads[0].wait()
    loads[1].wait()
    free = lax.dot_general(tab[...], pan[...], (((1,), (1,)), ((), ())), preferred_element_type=F32)
    for p in range(16):
        G[:, p, :48] = free[:, 48 * p : 48 * p + 48]
    force = lax.dot_general(
        G[...].reshape(128, 128)[:, :48], stiff, (((1,), (1,)), ((), ())),
        precision=lax.Precision.HIGHEST, preferred_element_type=F32,
    )
    picked = jnp.dot(pick, two_parts(force), preferred_element_type=F32)
    picked = jnp.concatenate([picked, jnp.zeros((192, 80), F32)], axis=1)
    lane24 = lax.broadcasted_iota(jnp.int32, (24, 128), 1)
    for c in range(3):
        message = jnp.zeros((24, 128), F32)
        for sn in range(8):
            part = picked[24 * sn : 24 * sn + 24]
            shift = (16 * (sn - c)) % 128
            if shift:
                part = pltpu.roll(part, shift, 1)
            message = jnp.where(lane24 // 16 == sn, part, message)
        msend[:, c, :] = message
    mrecv[gy] = msend[gy]

    near = 1 + has_left.astype(jnp.int32) + has_right.astype(jnp.int32) + has_up.astype(jnp.int32)
    loads[5].wait()
    pl.semaphore_wait(barrier, gy + near)

    def message_copy(peer, sender):
        return pltpu.make_async_remote_copy(
            src_ref=msend.at[peer], dst_ref=mrecv.at[sender], send_sem=fsend_sem.at[peer],
            recv_sem=frecv_sem.at[sender], device_id={"gy": peer}, device_id_type=MESH,
        )

    def x_copy(step, side):
        return pltpu.make_async_remote_copy(
            src_ref=U.at[step, :, 1 + 15 * side, 8:24], dst_ref=U.at[step, :, 17 - 17 * side, 8:24],
            send_sem=x_send.at[step, side], recv_sem=x_recv.at[step, side],
            device_id={"gx": gx - 1 + 2 * side}, device_id_type=MESH,
        )

    def y_copy(step, side):
        here, there = 8 + 15 * side, 24 - 17 * side
        return pltpu.make_async_remote_copy(
            src_ref=U.at[step, :, 1:17, here : here + 1], dst_ref=U.at[step, :, 1:17, there : there + 1],
            send_sem=y_send.at[step, side], recv_sem=y_recv.at[step, side],
            device_id={"gy": gy - 1 + 2 * side}, device_id_type=MESH,
        )

    def z_copy(step):
        return pltpu.make_async_remote_copy(
            src_ref=zsend.at[step], dst_ref=zrecv.at[step], send_sem=z_send.at[step], recv_sem=z_recv.at[step],
            device_id={"gz": 1 - gz}, device_id_type=MESH,
        )

    def start_x(step):
        for side, there in ((0, has_left), (1, has_right)):
            pl.when(there)(lambda side=side: x_copy(step, side).start())

    def start_yz(step):
        for side, there in ((0, has_down), (1, has_up)):
            pl.when(there)(lambda side=side: y_copy(step, side).start())
        z_copy(step).start()

    def wait_faces(step):
        for side, there in ((0, has_up), (1, has_down)):
            pl.when(there)(lambda side=side: y_copy(step, side).wait_recv())
        z_copy(step).wait_recv()
        for side, there in ((0, has_right), (1, has_left)):
            pl.when(there)(lambda side=side: x_copy(step, side).wait_recv())

    def wait_sent(step):
        for side, there in ((0, has_left), (1, has_right)):
            pl.when(there)(lambda side=side: x_copy(step, side).wait_send())
        for side, there in ((0, has_down), (1, has_up)):
            pl.when(there)(lambda side=side: y_copy(step, side).wait_send())
        z_copy(step).wait_send()

    def pack(place, value, packed):
        turned = pltpu.roll(value, place, 1) if place else value
        return jnp.where(lane16 == jnp.bitwise_and(edge + place, 127), turned, packed)

    start_x(0)

    @pl.loop(0, gy)
    def _(peer):
        message_copy(peer, gy).start()

    packed = jnp.zeros((16, 128), F32)
    for c in range(3):
        for x in range(16):
            packed = pack(16 * c + x, U[0, c, x + 1, 8:24], packed)
    zsend[0] = packed
    start_yz(0)

    loads[3].wait()
    k48 = lax.broadcasted_iota(jnp.int32, (48, 384), 0)
    q48 = lax.broadcasted_iota(jnp.int32, (48, 384), 1)
    late = k48 >= 32
    slot = jnp.where(late, (k48 - 32) // 8, k48 // 16)
    src = jnp.where(late, 16 + k48 % 8, k48 % 16)
    mine = jnp.logical_and(own[...] == gy + 64 * slot, q48 // 16 == src)
    slot_block = jnp.sum(jnp.where(mine, blk[...] + 1, 0), axis=1, keepdims=True) - 1
    column = lax.shift_right_arithmetic(slot_block, 3)
    hot = jnp.where(column == lax.broadcasted_iota(jnp.int32, (48, 256), 1), 1.0, 0.0)
    hot = jnp.transpose(jnp.concatenate([hot, jnp.zeros((80, 256), F32)], axis=0)).astype(BF16)
    hot_early = jnp.concatenate([hot[:, :32], hot[:, :32]], axis=1)
    hot_late = jnp.concatenate([hot[:, 32:48], hot[:, 32:48]], axis=1)

    for copy in loads[6:]:
        copy.wait()
    speed = jnp.zeros((1, 128), F32)
    for layer in range(spd.shape[1]):
        speed = jnp.where(dep[...] == layer, spd[0:1, layer : layer + 1], speed)
    lat[...] = lat[...] * speed[None]

    def turned_rows(first, count, at):
        out = []
        for s in range(2):
            zb = jnp.bitwise_and(slot_block[at + count * s : at + count * (s + 1)], 7)
            for c in range(3):
                row = mrecv[first : first + count, c, :]
                for b in range(3):
                    row = jnp.where(jnp.bitwise_and(zb, 1 << b) > 0, pltpu.roll(row, 16 << b, 1), row)
                out.append((s, c, zb, row))
        return out

    def placed(rows, count, hot, n):
        lanes = lax.broadcasted_iota(jnp.int32, (count, 128), 1) // 16
        parts = [[], []]
        for s, c, zb, row in rows:
            shift = (-16 * (4 * s + n)) % 128
            moved = pltpu.roll(row, shift, 1) if shift else row
            parts[s].append(jnp.where(lanes == zb, moved, 0.0))
        w = jnp.concatenate([jnp.concatenate(part, axis=1) for part in parts], axis=0)
        return jnp.dot(hot, two_parts(w), preferred_element_type=F32)

    def stencil(step, c, x, halo):
        v = U[step, c, x + 1, 8:24]
        place = 16 * c + x
        turned = pltpu.roll(halo, (128 - place) % 128, 1) if place else halo
        z = (
            jnp.where(at_low, 0.0, pltpu.roll(v, 1, 1))
            + jnp.where(at_high, 0.0, pltpu.roll(v, 127, 1))
            + jnp.where(at_edge, turned, 0.0)
        )
        y = U[step, c, x + 1, 7:23] + U[step, c, x + 1, 9:25]
        around = (U[step, c, x, 8:24] + U[step, c, x + 2, 8:24]) + y + z
        old = up[c, x] if step == 0 else U[step - 1, c, x + 1, 8:24]
        return (2.0 * v - old) + lat[x] * (around - 6.0 * v)

    order = [0, 15] + list(range(1, 15))

    def halo_of(step):
        return pltpu.roll(zrecv[step], jnp.bitwise_and(127 + 2 * gz, 127), 1)

    wait_faces(0)
    halo = halo_of(0)
    for x in order:
        for c in range(3):
            U[1, c, x + 1, 8:24] = stencil(0, c, x, halo)

    def message_wait(peer):
        message_copy(peer, peer).wait_recv()

    def message_reply(peer):
        message_copy(peer, peer).wait_recv()
        message_copy(peer, gy).start()

    turn = jnp.where(gy < 16, 16, n_gy)
    pl.loop(gy + 1, turn)(message_reply)
    pl.loop(0, jnp.minimum(gy, 16))(message_wait)
    rows = turned_rows(0, 16, 0)
    for n in range(NSTEP):
        D[n] = placed(rows, 16, hot_early, n)
    pl.loop(turn, n_gy)(message_reply)
    pl.loop(16, gy)(message_wait)
    rows = turned_rows(16, 8, 32)
    drive = D[0] + placed(rows, 8, hot_late, 0)
    packed = jnp.zeros((16, 128), F32)
    for x in order:
        for c in range(3):
            new = U[1, c, x + 1, 8:24] + drive[16 * x : 16 * x + 16, 128 * c : 128 * c + 128]
            U[1, c, x + 1, 8:24] = new
            packed = pack(16 * c + x, new, packed)
        if x == 15:
            start_x(1)
    zsend[1] = packed
    start_yz(1)
    for n in range(1, NSTEP):
        D[n] = D[n] + placed(rows, 8, hot_late, n)

    for step in range(1, NSTEP):
        wait_faces(step)
        halo = halo_of(step)
        packed = jnp.zeros((16, 128), F32)
        for x in order:
            for c in range(3):
                drive = D[step, 16 * x : 16 * x + 16, 128 * c : 128 * c + 128]
                new = stencil(step, c, x, halo) + drive
                if step < NSTEP - 1:
                    U[step + 1, c, x + 1, 8:24] = new
                    packed = pack(16 * c + x, new, packed)
                    if step == NSTEP - 2:
                        out_prev[c, x] = new
                else:
                    out_now[c, x] = new
            if step < NSTEP - 1 and x == 15:
                start_x(step + 1)
        if step < NSTEP - 1:
            zsend[step + 1] = packed
            start_yz(step + 1)

    for step in range(NSTEP):
        wait_sent(step)

    @pl.loop(1, n_gy)
    def _(k):
        message_copy(lax.rem(gy + k, n_gy), gy).wait_send()


def per_device(n_gx, n_gy, u_now, u_prev, panels, panel_owner, panel_block, coupling, layer_depth, layer_speed, lateral):
    spectral = panels.shape[4]
    count = panel_owner.shape[2]
    layers = layer_speed.shape[0]
    table = jnp.asarray(wave_table(spectral))
    anywhere = pl.BlockSpec(memory_space=pl.ANY)
    vmem = pl.BlockSpec(memory_space=pltpu.VMEM)
    dma = pltpu.SemaphoreType.DMA
    return pl.pallas_call(
        functools.partial(kernel, n_gx, n_gy),
        out_shape=(pltpu.VMEM(u_now.shape, F32), pltpu.VMEM(u_now.shape, F32)),
        in_specs=[anywhere] * 10,
        out_specs=(vmem, vmem),
        scratch_shapes=[
            pltpu.VMEM((NSTEP, 3, 18, 32, 128), F32),
            pltpu.VMEM(u_prev.shape, F32),
            pltpu.VMEM((768, spectral), BF16),
            pltpu.VMEM((1, count), jnp.int32),
            pltpu.VMEM((1, count), jnp.int32),
            pltpu.VMEM(coupling.shape, F32),
            pltpu.VMEM((1, 128), jnp.int32),
            pltpu.VMEM((1, layers), F32),
            pltpu.VMEM(lateral.shape, F32),
            pltpu.VMEM(table.shape, BF16),
            pltpu.VMEM((8, 16, 128), F32),
            pltpu.VMEM((NSTEP, 256, 384), F32),
            pltpu.VMEM((24, 3, 128), F32),
            pltpu.VMEM((24, 3, 128), F32),
            pltpu.VMEM((NSTEP, 16, 128), F32),
            pltpu.VMEM((NSTEP, 16, 128), F32),
            dma((10,)),
            dma((24,)),
            dma((24,)),
            dma((NSTEP, 2)),
            dma((NSTEP, 2)),
            dma((NSTEP, 2)),
            dma((NSTEP, 2)),
            dma((NSTEP,)),
            dma((NSTEP,)),
        ],
        compiler_params=pltpu.CompilerParams(collective_id=0, has_side_effects=True),
        name="domain_reduction",
    )(
        u_now, u_prev, panels.reshape(768, spectral), panel_owner.reshape(1, count), panel_block.reshape(1, count),
        coupling, layer_depth.reshape(1, 128), layer_speed.reshape(1, layers), lateral, table,
    )


def solution(mesh):
    in_specs = (
        P(None, "gx", "gy", "gz"),
        P(None, "gx", "gy", "gz"),
        P("gx", "gz", "gy", None, None),
        P("gx", "gz", None, None),
        P("gx", "gz", None),
        P(),
        P("gz"),
        P(),
        P("gx", "gy", "gz"),
    )
    out_specs = (P(None, "gx", "gy", "gz"), P(None, "gx", "gy", "gz"))
    return jax.shard_map(
        functools.partial(per_device, mesh.shape["gx"], mesh.shape["gy"]),
        mesh=mesh, in_specs=in_specs, out_specs=out_specs, check_vma=False,
    )
```

```python
import functools

import jax
import jax.numpy as jnp
import ml_dtypes
import numpy as np
from jax import lax
from jax.experimental import pallas as pl
from jax.experimental.pallas import tpu as pltpu
from jax.sharding import PartitionSpec as P

NSTEP = 4
MESH = pl.DeviceIdType.MESH
F32 = jnp.float32
BF16 = jnp.bfloat16


def wave_table(count):
    half = count // 2
    freq = np.float32(2.0 * np.pi) * (np.arange(half, dtype=np.float32) + np.float32(0.5)) / np.float32(count)
    times = np.float32(37.0) + np.arange(NSTEP, dtype=np.float32)
    phase = (freq[:, None] * times[None, :]).astype(np.float32)
    table = np.concatenate([np.cos(phase), np.sin(phase)], axis=0) / np.sqrt(np.float32(half))
    table = np.pad(table.T, ((0, 8 - NSTEP), (0, 0)))
    return table.astype(ml_dtypes.bfloat16)


def two_parts(b):
    hi = b.astype(BF16)
    lo = (b - hi.astype(F32)).astype(BF16)
    return jnp.concatenate([hi, lo], axis=0)


def kernel(
    n_gx, n_gy, u_hbm, up_hbm, pan_hbm, own_hbm, blk_hbm, cpl_hbm, dep_hbm, spd_hbm, lat_hbm, tab_hbm,
    out_now, out_prev,
    U, up, pan, own, blk, cpl, dep, spd, lat, tab, G, D, msend, mrecv,
    rate, D1, D1x, zsend, zrecv, zside, zrow, in_sem, fsend_sem, frecv_sem, send_sem, recv_sem,
):
    gx, gy, gz = lax.axis_index("gx"), lax.axis_index("gy"), lax.axis_index("gz")
    loads = [
        pltpu.make_async_copy(pan_hbm, pan, in_sem.at[0]),
        pltpu.make_async_copy(tab_hbm, tab, in_sem.at[1]),
        pltpu.make_async_copy(own_hbm, own, in_sem.at[2]),
        pltpu.make_async_copy(blk_hbm, blk, in_sem.at[3]),
        pltpu.make_async_copy(cpl_hbm, cpl, in_sem.at[4]),
        pltpu.make_async_copy(u_hbm, U.at[0, :, 2:18, 16:32], in_sem.at[5]),
        pltpu.make_async_copy(up_hbm, up, in_sem.at[6]),
        pltpu.make_async_copy(lat_hbm, lat.at[1:17, 16:32], in_sem.at[7]),
        pltpu.make_async_copy(dep_hbm, dep, in_sem.at[8]),
        pltpu.make_async_copy(spd_hbm, spd, in_sem.at[9]),
    ]
    for at in (2, 0, 1, 3, 4, 5, 6, 7, 8, 9):
        loads[at].start()

    barrier = pltpu.get_barrier_semaphore()

    has_left, has_right = gx > 0, gx < n_gx - 1
    has_down, has_up = gy > 0, gy < n_gy - 1

    def exists(dx, dy):
        there = gx >= 0
        if dx:
            there = has_right if dx > 0 else has_left
        if dy:
            there = jnp.logical_and(there, has_up if dy > 0 else has_down)
        return there

    def device(dx, dy, dz):
        return {"gx": gx + dx, "gy": gy + dy, "gz": 1 - gz if dz else gz}

    near = [
        (dx, dy, 0) for dx in (-1, 0, 1) for dy in (-1, 0, 1) if dx or dy
    ] + [(0, 0, 1), (-1, 0, 1), (1, 0, 1), (0, -1, 1), (0, 1, 1)]
    count = gy
    for dx, dy, dz in near:
        if (dx, dy, dz) != (0, 1, 0):
            pl.when(exists(dx, dy))(
                lambda to=(dx, dy, dz): pl.semaphore_signal(
                    barrier, inc=1, device_id=device(*to), device_id_type=MESH
                )
            )
        if (dx, dy, dz) != (0, -1, 0):
            count = count + exists(dx, dy).astype(jnp.int32)

    @pl.loop(gy + 1, n_gy)
    def _(peer):
        pl.semaphore_signal(barrier, inc=1, device_id={"gy": peer}, device_id_type=MESH)

    @pl.when(jnp.logical_not(has_left))
    def _():
        U[:, :, 0:2, 8:40] = jnp.zeros((NSTEP, 3, 2, 32, 128), F32)
        lat[0, 16:32] = jnp.zeros((16, 128), F32)
        D1x[0] = jnp.zeros((16, 384), F32)
        zside[0] = jnp.zeros((16, 128), F32)

    @pl.when(jnp.logical_not(has_right))
    def _():
        U[:, :, 18:20, 8:40] = jnp.zeros((NSTEP, 3, 2, 32, 128), F32)
        lat[17, 16:32] = jnp.zeros((16, 128), F32)
        D1x[1] = jnp.zeros((16, 384), F32)
        zside[1] = jnp.zeros((16, 128), F32)

    @pl.when(jnp.logical_not(has_down))
    def _():
        U[:, :, :, 8:16] = jnp.zeros((NSTEP, 3, 20, 8, 128), F32)
        lat[1:17, 8:16] = jnp.zeros((16, 8, 128), F32)
        D1[:, 8:16] = jnp.zeros((16, 8, 384), F32)
        zrow[0] = jnp.zeros((8, 128), F32)

    @pl.when(jnp.logical_not(has_up))
    def _():
        U[:, :, :, 32:40] = jnp.zeros((NSTEP, 3, 20, 8, 128), F32)
        lat[1:17, 32:40] = jnp.zeros((16, 8, 128), F32)
        D1[:, 32:40] = jnp.zeros((16, 8, 384), F32)
        zrow[1] = jnp.zeros((8, 128), F32)

    edge = 127 - 127 * gz
    lane16 = lax.broadcasted_iota(jnp.int32, (16, 128), 1)

    loads[2].wait()
    owner = own[...]
    q = lax.broadcasted_iota(jnp.int32, (1, 384), 1)
    rank = jnp.zeros((1, 384), jnp.int32)
    for d in range(1, 16):
        same = jnp.logical_and(q % 16 >= d, pltpu.roll(owner, d, 1) == owner)
        rank = rank + same.astype(jnp.int32)
    own[...] = owner + 64 * rank

    tile = gy // 8
    off = (gy - 8 * tile) * 16
    lane1 = lax.broadcasted_iota(jnp.int32, (1, 128), 1)
    mycode = own[:, pl.ds(pl.multiple_of(tile * 128, 128), 128)]
    mycode = jnp.where(jnp.logical_and(lane1 >= off, lane1 < off + 16), mycode, 0)
    for s in (16, 32, 64):
        mycode = mycode + pltpu.roll(mycode, s, 1)
    r192 = lax.broadcasted_iota(jnp.int32, (192, 128), 0)
    l192 = lax.broadcasted_iota(jnp.int32, (192, 128), 1)
    want = (r192 % 24) + 64 * (r192 // 96)
    step_of = (r192 // 24) % 4
    pick = jnp.where(jnp.logical_and(mycode == want, l192 // 16 == step_of), 1.0, 0.0).astype(BF16)
    pick = jnp.concatenate([pick, pick], axis=1)

    G[...] = jnp.zeros_like(G)
    loads[4].wait()
    zero = jnp.zeros((16, 16), F32)
    stiff = jnp.concatenate(
        [jnp.concatenate([cpl[c] if c == k else zero for k in range(3)], axis=1) for c in range(3)], axis=0
    )
    loads[0].wait()
    loads[1].wait()
    free = lax.dot_general(tab[...], pan[...], (((1,), (1,)), ((), ())), preferred_element_type=F32)
    for p in range(16):
        G[:, p, :48] = free[:, 48 * p : 48 * p + 48]
    force = lax.dot_general(
        G[...].reshape(128, 128)[:, :48], stiff, (((1,), (1,)), ((), ())),
        precision=lax.Precision.HIGHEST, preferred_element_type=F32,
    )
    picked = jnp.dot(pick, two_parts(force), preferred_element_type=F32)
    picked = jnp.concatenate([picked, jnp.zeros((192, 80), F32)], axis=1)
    lane24 = lax.broadcasted_iota(jnp.int32, (24, 128), 1)
    for c in range(3):
        message = jnp.zeros((24, 128), F32)
        for sn in range(8):
            part = picked[24 * sn : 24 * sn + 24]
            shift = (16 * (sn - c)) % 128
            if shift:
                part = pltpu.roll(part, shift, 1)
            message = jnp.where(lane24 // 16 == sn, part, message)
        msend[:, c, :] = message
    mrecv[gy] = msend[gy]

    loads[5].wait()
    loads[7].wait()
    pl.semaphore_wait(barrier, count)

    def message_copy(peer, sender):
        return pltpu.make_async_remote_copy(
            src_ref=msend.at[peer], dst_ref=mrecv.at[sender], send_sem=fsend_sem.at[peer],
            recv_sem=frecv_sem.at[sender], device_id={"gy": peer}, device_id_type=MESH,
        )

    def exchange(first, moves):
        return [
            (
                to,
                pltpu.make_async_remote_copy(
                    src_ref=src, dst_ref=dst, send_sem=send_sem.at[first + k], recv_sem=recv_sem.at[first + k],
                    device_id=device(*to), device_id_type=MESH,
                ),
            )
            for k, (to, src, dst) in enumerate(moves)
        ]

    def start(copies):
        for to, copy in copies:
            pl.when(exists(to[0], to[1]))(copy.start)

    def arrive(copies):
        for to, copy in copies:
            pl.when(exists(-to[0], -to[1]))(copy.wait_recv)

    def sent(copies):
        for to, copy in copies:
            pl.when(exists(to[0], to[1]))(copy.wait_send)

    def x_faces(step, width):
        return [
            ((-1, 0, 0), U.at[step, :, 2 : 2 + width, 16:32], U.at[step, :, 18 : 18 + width, 16:32]),
            ((1, 0, 0), U.at[step, :, 18 - width : 18, 16:32], U.at[step, :, 2 - width : 2, 16:32]),
        ]

    def y_faces(step, width):
        return [
            ((0, -1, 0), U.at[step, :, 2:18, 16 : 16 + width], U.at[step, :, 2:18, 32 : 32 + width]),
            ((0, 1, 0), U.at[step, :, 2:18, 32 - width : 32], U.at[step, :, 2:18, 16 - width : 16]),
        ]

    first_x = exchange(0, x_faces(0, 1))
    first_yz = exchange(2, y_faces(0, 1) + [
        ((0, 0, 1), zsend.at[0:2], zrecv.at[0:2]),
        ((-1, 0, 0), lat.at[1, 16:32], lat.at[17, 16:32]),
        ((1, 0, 0), lat.at[16, 16:32], lat.at[0, 16:32]),
        ((0, -1, 0), lat.at[1:17, 16:17], lat.at[1:17, 32:33]),
        ((0, 1, 0), lat.at[1:17, 31:32], lat.at[1:17, 15:16]),
    ])
    deep_x = exchange(9, x_faces(1, 2) + [
        ((-1, 0, 0), D1.at[0, 16:32], D1x.at[1]),
        ((1, 0, 0), D1.at[15, 16:32], D1x.at[0]),
    ])
    deep_y = exchange(13, [
        ((dx, dy, 0), U.at[1, :, 2 if dx < 0 else 17, pl.ds(16 if dy < 0 else 31, 1)],
         U.at[1, :, 18 if dx < 0 else 1, pl.ds(32 if dy < 0 else 15, 1)])
        for dx in (-1, 1) for dy in (-1, 1)
    ] + y_faces(1, 2) + [
        ((0, -1, 0), D1.at[:, 16:17], D1.at[:, 32:33]),
        ((0, 1, 0), D1.at[:, 31:32], D1.at[:, 15:16]),
    ])
    deep_z = exchange(21, [
        ((-1, 0, 1), zsend.at[2], zside.at[1]),
        ((1, 0, 1), zsend.at[2], zside.at[0]),
        ((0, -1, 1), zsend.at[2, 0:8], zrow.at[1]),
        ((0, 1, 1), zsend.at[2, 8:16], zrow.at[0]),
        ((0, 0, 1), zsend.at[2:5], zrecv.at[2:5]),
    ])
    last_x = exchange(26, x_faces(3, 1))
    last_yz = exchange(28, y_faces(3, 1) + [((0, 0, 1), zsend.at[5], zrecv.at[5])])

    def pack(place, value, packed):
        turned = pltpu.roll(value, place, 1) if place else value
        return jnp.where(lane16 == jnp.bitwise_and(edge + place, 127), turned, packed)

    start(first_x)

    @pl.loop(0, gy)
    def _(peer):
        message_copy(peer, gy).start()

    for copy in (loads[8], loads[9]):
        copy.wait()
    speed = jnp.zeros((1, 128), F32)
    for layer in range(spd.shape[1]):
        speed = jnp.where(dep[...] == layer, spd[0:1, layer : layer + 1], speed)
    rate[1:17, 16:32] = lat[1:17, 16:32] * speed[None]
    packed, packed_rate = jnp.zeros((16, 128), F32), jnp.zeros((16, 128), F32)
    for c in range(3):
        for x in range(16):
            packed = pack(16 * c + x, U[0, c, x + 2, 16:32], packed)
            packed_rate = pack(16 * c + x, rate[x + 1, 16:32], packed_rate)
    zsend[0] = packed
    zsend[1] = packed_rate
    start(first_yz)

    loads[3].wait()
    k48 = lax.broadcasted_iota(jnp.int32, (48, 384), 0)
    q48 = lax.broadcasted_iota(jnp.int32, (48, 384), 1)
    late = k48 >= 32
    slot = jnp.where(late, (k48 - 32) // 8, k48 // 16)
    src = jnp.where(late, 16 + k48 % 8, k48 % 16)
    mine = jnp.logical_and(own[...] == gy + 64 * slot, q48 // 16 == src)
    slot_block = jnp.sum(jnp.where(mine, blk[...] + 1, 0), axis=1, keepdims=True) - 1
    column = lax.shift_right_arithmetic(slot_block, 3)
    hot = jnp.where(column == lax.broadcasted_iota(jnp.int32, (48, 256), 1), 1.0, 0.0)
    hot = jnp.transpose(jnp.concatenate([hot, jnp.zeros((80, 256), F32)], axis=0)).astype(BF16)
    hot_early = jnp.concatenate([hot[:, :32], hot[:, :32]], axis=1)
    hot_late = jnp.concatenate([hot[:, 32:48], hot[:, 32:48]], axis=1)

    loads[6].wait()

    def turned_rows(first, count, at):
        out = []
        for s in range(2):
            zb = jnp.bitwise_and(slot_block[at + count * s : at + count * (s + 1)], 7)
            for c in range(3):
                row = mrecv[first : first + count, c, :]
                for b in range(3):
                    row = jnp.where(jnp.bitwise_and(zb, 1 << b) > 0, pltpu.roll(row, 16 << b, 1), row)
                out.append((s, c, zb, row))
        return out

    def placed(rows, count, hot, n):
        lanes = lax.broadcasted_iota(jnp.int32, (count, 128), 1) // 16
        parts = [[], []]
        for s, c, zb, row in rows:
            shift = (-16 * (4 * s + n)) % 128
            moved = pltpu.roll(row, shift, 1) if shift else row
            parts[s].append(jnp.where(lanes == zb, moved, 0.0))
        w = jnp.concatenate([jnp.concatenate(part, axis=1) for part in parts], axis=0)
        return jnp.dot(hot, two_parts(w), preferred_element_type=F32)

    def stencil(step, c, x, halo, lo=16, rows=16):
        here = pl.ds(lo, rows)
        v = U[step, c, x + 2, here]
        lanes = lax.broadcasted_iota(jnp.int32, (rows, 128), 1)
        z = (
            jnp.where(lanes == 0, 0.0, pltpu.roll(v, 1, 1))
            + jnp.where(lanes == 127, 0.0, pltpu.roll(v, 127, 1))
            + jnp.where(lanes == edge, halo, 0.0)
        )
        y = U[step, c, x + 2, pl.ds(lo - 1, rows)] + U[step, c, x + 2, pl.ds(lo + 1, rows)]
        around = (U[step, c, x + 1, here] + U[step, c, x + 3, here]) + y + z
        old = up[c, x] if step == 0 else U[step - 1, c, x + 2, here]
        return (2.0 * v - old) + rate[x + 1, here] * (around - 6.0 * v)

    def to_edge(packed, place):
        return pltpu.roll(packed, 128 - place, 1) if place else packed

    order = [0, 15, 1, 14] + list(range(2, 14))

    def received(packed):
        return pltpu.roll(packed, jnp.bitwise_and(127 + 2 * gz, 127), 1)

    arrive(first_yz)
    arrive(first_x)
    rate[0:1, 16:32] = lat[0:1, 16:32] * speed[None]
    rate[17:18, 16:32] = lat[17:18, 16:32] * speed[None]
    rate[1:17, 8:16] = lat[1:17, 8:16] * speed[None]
    rate[1:17, 32:40] = lat[1:17, 32:40] * speed[None]
    halo0 = received(zrecv[0])
    for x in order:
        for c in range(3):
            U[1, c, x + 2, 16:32] = stencil(0, c, x, to_edge(halo0, 16 * c + x))

    def message_wait(peer):
        message_copy(peer, peer).wait_recv()

    def message_reply(peer):
        message_copy(peer, peer).wait_recv()
        message_copy(peer, gy).start()

    turn = jnp.where(gy < 16, 16, n_gy)
    pl.loop(gy + 1, turn)(message_reply)
    pl.loop(0, jnp.minimum(gy, 16))(message_wait)
    rows = turned_rows(0, 16, 0)
    D[0] = placed(rows, 16, hot_early, 0)
    D1[:, 16:32] = placed(rows, 16, hot_early, 1).reshape(16, 16, 384)
    for n in (2, 3):
        D[n - 1] = placed(rows, 16, hot_early, n)
    pl.loop(turn, n_gy)(message_reply)
    pl.loop(16, gy)(message_wait)
    rows = turned_rows(16, 8, 32)
    drive = D[0] + placed(rows, 8, hot_late, 0)
    D1[:, 16:32] = D1[:, 16:32] + placed(rows, 8, hot_late, 1).reshape(16, 16, 384)
    edge_1 = inner_1 = edge_d = jnp.zeros((16, 128), F32)
    inward = jnp.where(gz == 0, 1, 127)
    for x in order:
        for c in range(3):
            new = U[1, c, x + 2, 16:32] + drive[16 * x : 16 * x + 16, 128 * c : 128 * c + 128]
            U[1, c, x + 2, 16:32] = new
            edge_1 = pack(16 * c + x, new, edge_1)
            inner_1 = pack(16 * c + x, pltpu.roll(new, inward, 1), inner_1)
            edge_d = pack(16 * c + x, D1[x, 16:32, 128 * c : 128 * c + 128], edge_d)
        if x == 14:
            start(deep_x)
    zsend[2] = edge_1
    zsend[3] = inner_1
    zsend[4] = edge_d
    start(deep_y)
    start(deep_z)
    for n in (2, 3):
        D[n - 1] = D[n - 1] + placed(rows, 8, hot_late, n)

    arrive(deep_z)
    arrive(deep_y)
    arrive(deep_x)
    halo1 = received(zrecv[2])
    left1, right1 = received(zside[0]), received(zside[1])
    tall = received(jnp.concatenate([zrow[0], zrecv[2], zrow[1]], axis=0))[4:28]
    for c in range(3):
        U[2, c, 1, 16:32] = stencil(1, c, -1, to_edge(left1, 16 * c + 15)) + D1x[0, :, 128 * c : 128 * c + 128]
        U[2, c, 18, 16:32] = stencil(1, c, 16, to_edge(right1, 16 * c)) + D1x[1, :, 128 * c : 128 * c + 128]
        for x in range(16):
            U[2, c, x + 2, 12:36] = (
                stencil(1, c, x, to_edge(tall, 16 * c + x), 12, 24) + D1[x, 12:36, 128 * c : 128 * c + 128]
            )
    x_of = jnp.bitwise_and(lane16 - edge, 15)
    row16 = lax.broadcasted_iota(jnp.int32, (16, 128), 0)
    beside = (
        jnp.where(x_of == 0, pltpu.roll(left1, 113, 1), pltpu.roll(halo1, 1, 1))
        + jnp.where(x_of == 15, pltpu.roll(right1, 15, 1), pltpu.roll(halo1, 127, 1))
        + tall[3:19] + tall[5:21] + edge_1 + received(zrecv[3])
    )
    halo = (2.0 * halo1 - halo0) + received(zrecv[1]) * (beside - 6.0 * halo1) + received(zrecv[4])

    packed = jnp.zeros((16, 128), F32)
    for x in order:
        for c in range(3):
            drive = D[1, 16 * x : 16 * x + 16, 128 * c : 128 * c + 128]
            new = stencil(2, c, x, to_edge(halo, 16 * c + x)) + drive
            U[3, c, x + 2, 16:32] = new
            packed = pack(16 * c + x, new, packed)
            out_prev[c, x] = new
        if x == 15:
            start(last_x)
    zsend[5] = packed
    start(last_yz)

    arrive(last_yz)
    arrive(last_x)
    halo = received(zrecv[5])
    for x in order:
        for c in range(3):
            drive = D[2, 16 * x : 16 * x + 16, 128 * c : 128 * c + 128]
            out_now[c, x] = stencil(3, c, x, to_edge(halo, 16 * c + x)) + drive

    for copies in (first_x, first_yz, deep_x, deep_y, deep_z, last_x, last_yz):
        sent(copies)

    @pl.loop(1, n_gy)
    def _(k):
        message_copy(lax.rem(gy + k, n_gy), gy).wait_send()


def per_device(n_gx, n_gy, u_now, u_prev, panels, panel_owner, panel_block, coupling, layer_depth, layer_speed, lateral):
    spectral = panels.shape[4]
    count = panel_owner.shape[2]
    layers = layer_speed.shape[0]
    table = jnp.asarray(wave_table(spectral))
    anywhere = pl.BlockSpec(memory_space=pl.ANY)
    vmem = pl.BlockSpec(memory_space=pltpu.VMEM)
    dma = pltpu.SemaphoreType.DMA
    return pl.pallas_call(
        functools.partial(kernel, n_gx, n_gy),
        out_shape=(pltpu.VMEM(u_now.shape, F32), pltpu.VMEM(u_now.shape, F32)),
        in_specs=[anywhere] * 10,
        out_specs=(vmem, vmem),
        scratch_shapes=[
            pltpu.VMEM((NSTEP, 3, 20, 48, 128), F32),
            pltpu.VMEM(u_prev.shape, F32),
            pltpu.VMEM((768, spectral), BF16),
            pltpu.VMEM((1, count), jnp.int32),
            pltpu.VMEM((1, count), jnp.int32),
            pltpu.VMEM(coupling.shape, F32),
            pltpu.VMEM((1, 128), jnp.int32),
            pltpu.VMEM((1, layers), F32),
            pltpu.VMEM((18, 48, 128), F32),
            pltpu.VMEM(table.shape, BF16),
            pltpu.VMEM((8, 16, 128), F32),
            pltpu.VMEM((3, 256, 384), F32),
            pltpu.VMEM((24, 3, 128), F32),
            pltpu.VMEM((24, 3, 128), F32),
            pltpu.VMEM((18, 48, 128), F32),
            pltpu.VMEM((16, 48, 384), F32),
            pltpu.VMEM((2, 16, 384), F32),
            pltpu.VMEM((6, 16, 128), F32),
            pltpu.VMEM((6, 16, 128), F32),
            pltpu.VMEM((2, 16, 128), F32),
            pltpu.VMEM((2, 8, 128), F32),
            dma((10,)),
            dma((24,)),
            dma((24,)),
            dma((31,)),
            dma((31,)),
        ],
        compiler_params=pltpu.CompilerParams(collective_id=0, has_side_effects=True),
        name="domain_reduction",
    )(
        u_now, u_prev, panels.reshape(768, spectral), panel_owner.reshape(1, count), panel_block.reshape(1, count),
        coupling, layer_depth.reshape(1, 128), layer_speed.reshape(1, layers), lateral, table,
    )


def solution(mesh):
    in_specs = (
        P(None, "gx", "gy", "gz"),
        P(None, "gx", "gy", "gz"),
        P("gx", "gz", "gy", None, None),
        P("gx", "gz", None, None),
        P("gx", "gz", None),
        P(),
        P("gz"),
        P(),
        P("gx", "gy", "gz"),
    )
    out_specs = (P(None, "gx", "gy", "gz"), P(None, "gx", "gy", "gz"))
    return jax.shard_map(
        functools.partial(per_device, mesh.shape["gx"], mesh.shape["gy"]),
        mesh=mesh, in_specs=in_specs, out_specs=out_specs, check_vma=False,
    )
```

```python
import functools

import jax
import jax.numpy as jnp
import ml_dtypes
import numpy as np
from jax import lax
from jax.experimental import pallas as pl
from jax.experimental.pallas import tpu as pltpu
from jax.sharding import PartitionSpec as P

NSTEP = 4
MESH = pl.DeviceIdType.MESH
F32 = jnp.float32
BF16 = jnp.bfloat16


def wave_table(count):
    half = count // 2
    freq = np.float32(2.0 * np.pi) * (np.arange(half, dtype=np.float32) + np.float32(0.5)) / np.float32(count)
    times = np.float32(37.0) + np.arange(NSTEP, dtype=np.float32)
    phase = (freq[:, None] * times[None, :]).astype(np.float32)
    table = np.concatenate([np.cos(phase), np.sin(phase)], axis=0) / np.sqrt(np.float32(half))
    table = np.pad(table.T, ((0, 8 - NSTEP), (0, 0)))
    return table.astype(ml_dtypes.bfloat16)


def two_parts(b):
    hi = b.astype(BF16)
    lo = (b - hi.astype(F32)).astype(BF16)
    return jnp.concatenate([hi, lo], axis=0)


def kernel(
    n_gx, n_gy, u_hbm, up_hbm, pan_hbm, own_hbm, blk_hbm, cpl_hbm, dep_hbm, spd_hbm, lat_hbm, tab_hbm,
    out_now, out_prev,
    U, up, pan, own, blk, cpl, dep, spd, lat, tab, G, D, msend, mrecv,
    rate, D1, D1x, zsend, zrecv, zside, zrow, in_sem, fsend_sem, frecv_sem, send_sem, recv_sem, known,
):
    gx, gy, gz = lax.axis_index("gx"), lax.axis_index("gy"), lax.axis_index("gz")
    loads = [
        pltpu.make_async_copy(pan_hbm, pan, in_sem.at[0]),
        pltpu.make_async_copy(tab_hbm, tab, in_sem.at[1]),
        pltpu.make_async_copy(own_hbm, own, in_sem.at[2]),
        pltpu.make_async_copy(blk_hbm, blk, in_sem.at[3]),
        pltpu.make_async_copy(cpl_hbm, cpl, in_sem.at[4]),
        pltpu.make_async_copy(u_hbm, U.at[0, :, 2:18, 16:32], in_sem.at[5]),
        pltpu.make_async_copy(up_hbm, up, in_sem.at[6]),
        pltpu.make_async_copy(lat_hbm, lat.at[1:17, 16:32], in_sem.at[7]),
        pltpu.make_async_copy(dep_hbm, dep, in_sem.at[8]),
        pltpu.make_async_copy(spd_hbm, spd, in_sem.at[9]),
    ]
    for at in (2, 0, 1, 3, 4, 5, 6, 7, 8, 9):
        loads[at].start()

    barrier = pltpu.get_barrier_semaphore()

    has_left, has_right = gx > 0, gx < n_gx - 1
    has_down, has_up = gy > 0, gy < n_gy - 1

    def exists(dx, dy):
        there = gx >= 0
        if dx:
            there = has_right if dx > 0 else has_left
        if dy:
            there = jnp.logical_and(there, has_up if dy > 0 else has_down)
        return there

    def device(dx, dy, dz):
        return {"gx": gx + dx, "gy": gy + dy, "gz": 1 - gz if dz else gz}

    middle = n_gx // 2
    lead_left = jnp.logical_and(has_left, gx != middle)
    lead_right = gx == middle - 1
    lead_z = gz == 1
    told_right = jnp.logical_and(has_right, gx != middle - 1)

    def tell(there, to):
        pl.when(there)(
            lambda: pl.semaphore_signal(barrier, inc=1, device_id=device(*to), device_id_type=MESH)
        )

    tell(gx == middle, (-1, 0, 0))
    tell(told_right, (1, 0, 0))
    lonely = jnp.logical_and(gy == 0, jnp.logical_or(gx == 0, gx == middle))
    tell(jnp.logical_or(gz == 0, lonely), (0, 0, 1))
    told_z = jnp.logical_or(lead_z, lonely)
    count = gy + lead_left.astype(jnp.int32) + lead_right.astype(jnp.int32) + told_z.astype(jnp.int32)

    @pl.loop(gy + 1, n_gy)
    def _(peer):
        pl.semaphore_signal(barrier, inc=1, device_id={"gy": peer}, device_id_type=MESH)

    @pl.when(jnp.logical_not(has_left))
    def _():
        U[:, :, 0:2, 8:40] = jnp.zeros((NSTEP, 3, 2, 32, 128), F32)
        lat[0, 16:32] = jnp.zeros((16, 128), F32)
        D1x[0] = jnp.zeros((16, 384), F32)
        zside[0] = jnp.zeros((16, 128), F32)

    @pl.when(jnp.logical_not(has_right))
    def _():
        U[:, :, 18:20, 8:40] = jnp.zeros((NSTEP, 3, 2, 32, 128), F32)
        lat[17, 16:32] = jnp.zeros((16, 128), F32)
        D1x[1] = jnp.zeros((16, 384), F32)
        zside[1] = jnp.zeros((16, 128), F32)

    @pl.when(jnp.logical_not(has_down))
    def _():
        U[:, :, :, 8:16] = jnp.zeros((NSTEP, 3, 20, 8, 128), F32)
        lat[1:17, 8:16] = jnp.zeros((16, 8, 128), F32)
        D1[:, 8:16] = jnp.zeros((16, 8, 384), F32)
        zrow[0] = jnp.zeros((8, 128), F32)

    @pl.when(jnp.logical_not(has_up))
    def _():
        U[:, :, :, 32:40] = jnp.zeros((NSTEP, 3, 20, 8, 128), F32)
        lat[1:17, 32:40] = jnp.zeros((16, 8, 128), F32)
        D1[:, 32:40] = jnp.zeros((16, 8, 384), F32)
        zrow[1] = jnp.zeros((8, 128), F32)

    edge = 127 - 127 * gz
    lane16 = lax.broadcasted_iota(jnp.int32, (16, 128), 1)

    loads[2].wait()
    owner = own[...]
    q = lax.broadcasted_iota(jnp.int32, (1, 384), 1)
    rank = jnp.zeros((1, 384), jnp.int32)
    for d in range(1, 16):
        same = jnp.logical_and(q % 16 >= d, pltpu.roll(owner, d, 1) == owner)
        rank = rank + same.astype(jnp.int32)
    own[...] = owner + 64 * rank

    tile = gy // 8
    off = (gy - 8 * tile) * 16
    lane1 = lax.broadcasted_iota(jnp.int32, (1, 128), 1)
    mycode = own[:, pl.ds(pl.multiple_of(tile * 128, 128), 128)]
    mycode = jnp.where(jnp.logical_and(lane1 >= off, lane1 < off + 16), mycode, 0)
    for s in (16, 32, 64):
        mycode = mycode + pltpu.roll(mycode, s, 1)
    r192 = lax.broadcasted_iota(jnp.int32, (192, 128), 0)
    l192 = lax.broadcasted_iota(jnp.int32, (192, 128), 1)
    want = (r192 % 24) + 64 * (r192 // 96)
    step_of = (r192 // 24) % 4
    pick = jnp.where(jnp.logical_and(mycode == want, l192 // 16 == step_of), 1.0, 0.0).astype(BF16)
    pick = jnp.concatenate([pick, pick], axis=1)

    G[...] = jnp.zeros_like(G)
    loads[4].wait()
    zero = jnp.zeros((16, 16), F32)
    stiff = jnp.concatenate(
        [jnp.concatenate([cpl[c] if c == k else zero for k in range(3)], axis=1) for c in range(3)], axis=0
    )
    loads[0].wait()
    loads[1].wait()
    free = lax.dot_general(tab[...], pan[...], (((1,), (1,)), ((), ())), preferred_element_type=F32)
    for p in range(16):
        G[:, p, :48] = free[:, 48 * p : 48 * p + 48]
    force = lax.dot_general(
        G[...].reshape(128, 128)[:, :48], stiff, (((1,), (1,)), ((), ())),
        precision=lax.Precision.HIGHEST, preferred_element_type=F32,
    )
    picked = jnp.dot(pick, two_parts(force), preferred_element_type=F32)
    picked = jnp.concatenate([picked, jnp.zeros((192, 80), F32)], axis=1)
    lane24 = lax.broadcasted_iota(jnp.int32, (24, 128), 1)
    for c in range(3):
        message = jnp.zeros((24, 128), F32)
        for sn in range(8):
            part = picked[24 * sn : 24 * sn + 24]
            shift = (16 * (sn - c)) % 128
            if shift:
                part = pltpu.roll(part, shift, 1)
            message = jnp.where(lane24 // 16 == sn, part, message)
        msend[:, c, :] = message
    mrecv[gy] = msend[gy]

    loads[5].wait()
    loads[7].wait()
    pl.semaphore_wait(barrier, count)

    def message_copy(peer, sender):
        return pltpu.make_async_remote_copy(
            src_ref=msend.at[peer], dst_ref=mrecv.at[sender], send_sem=fsend_sem.at[peer],
            recv_sem=frecv_sem.at[sender], device_id={"gy": peer}, device_id_type=MESH,
        )

    def exchange(first, moves):
        return [
            (
                to,
                pltpu.make_async_remote_copy(
                    src_ref=src, dst_ref=dst, send_sem=send_sem.at[first + k], recv_sem=recv_sem.at[first + k],
                    device_id=device(*to), device_id_type=MESH,
                ),
            )
            for k, (to, src, dst) in enumerate(moves)
        ]

    def start(copies):
        for to, copy in copies:
            pl.when(exists(to[0], to[1]))(copy.start)

    def arrive(copies):
        for to, copy in copies:
            pl.when(exists(-to[0], -to[1]))(copy.wait_recv)

    def sent(copies):
        for to, copy in copies:
            pl.when(exists(to[0], to[1]))(copy.wait_send)

    def x_faces(step, width):
        return [
            ((-1, 0, 0), U.at[step, :, 2 : 2 + width, 16:32], U.at[step, :, 18 : 18 + width, 16:32]),
            ((1, 0, 0), U.at[step, :, 18 - width : 18, 16:32], U.at[step, :, 2 - width : 2, 16:32]),
        ]

    def y_faces(step, width):
        return [
            ((0, -1, 0), U.at[step, :, 2:18, 16 : 16 + width], U.at[step, :, 2:18, 32 : 32 + width]),
            ((0, 1, 0), U.at[step, :, 2:18, 32 - width : 32], U.at[step, :, 2:18, 16 - width : 16]),
        ]

    (u_left, u_right), (u_down, u_up) = x_faces(0, 1), y_faces(0, 1)
    left = exchange(0, [u_left, ((-1, 0, 0), lat.at[1, 16:32], lat.at[17, 16:32])])
    right = exchange(2, [u_right, ((1, 0, 0), lat.at[16, 16:32], lat.at[0, 16:32])])
    down = exchange(4, [u_down, ((0, -1, 0), lat.at[1:17, 16:17], lat.at[1:17, 32:33])])
    up_gy = exchange(6, [u_up, ((0, 1, 0), lat.at[1:17, 31:32], lat.at[1:17, 15:16])])
    across = exchange(8, [((0, 0, 1), zsend.at[0:2], zrecv.at[0:2])])
    deep_x = exchange(9, x_faces(1, 2) + [
        ((-1, 0, 0), D1.at[0, 16:32], D1x.at[1]),
        ((1, 0, 0), D1.at[15, 16:32], D1x.at[0]),
    ])
    deep_y = exchange(13, [
        ((dx, dy, 0), U.at[1, :, 2 if dx < 0 else 17, pl.ds(16 if dy < 0 else 31, 1)],
         U.at[1, :, 18 if dx < 0 else 1, pl.ds(32 if dy < 0 else 15, 1)])
        for dx in (-1, 1) for dy in (-1, 1)
    ] + y_faces(1, 2) + [
        ((0, -1, 0), D1.at[:, 16:17], D1.at[:, 32:33]),
        ((0, 1, 0), D1.at[:, 31:32], D1.at[:, 15:16]),
    ])
    deep_z = exchange(21, [
        ((-1, 0, 1), zsend.at[2], zside.at[1]),
        ((1, 0, 1), zsend.at[2], zside.at[0]),
        ((0, -1, 1), zsend.at[2, 0:8], zrow.at[1]),
        ((0, 1, 1), zsend.at[2, 8:16], zrow.at[0]),
        ((0, 0, 1), zsend.at[2:5], zrecv.at[2:5]),
    ])
    last_x = exchange(26, x_faces(3, 1))
    last_yz = exchange(28, y_faces(3, 1) + [((0, 0, 1), zsend.at[5], zrecv.at[5])])

    def pack(place, value, packed):
        turned = pltpu.roll(value, place, 1) if place else value
        return jnp.where(lane16 == jnp.bitwise_and(edge + place, 127), turned, packed)

    @pl.loop(0, gy)
    def _(peer):
        message_copy(peer, gy).start()

    pl.when(lead_left)(lambda: start(left))
    pl.when(lead_right)(lambda: start(right))
    start(down)

    for copy in (loads[8], loads[9]):
        copy.wait()
    speed = jnp.zeros((1, 128), F32)
    for layer in range(spd.shape[1]):
        speed = jnp.where(dep[...] == layer, spd[0:1, layer : layer + 1], speed)
    rate[1:17, 16:32] = lat[1:17, 16:32] * speed[None]
    packed, packed_rate = jnp.zeros((16, 128), F32), jnp.zeros((16, 128), F32)
    for c in range(3):
        for x in range(16):
            packed = pack(16 * c + x, U[0, c, x + 2, 16:32], packed)
            packed_rate = pack(16 * c + x, rate[x + 1, 16:32], packed_rate)
    zsend[0] = packed
    zsend[1] = packed_rate
    pl.when(lead_z)(lambda: start(across))

    loads[3].wait()
    k48 = lax.broadcasted_iota(jnp.int32, (48, 384), 0)
    q48 = lax.broadcasted_iota(jnp.int32, (48, 384), 1)
    late = k48 >= 32
    slot = jnp.where(late, (k48 - 32) // 8, k48 // 16)
    src = jnp.where(late, 16 + k48 % 8, k48 % 16)
    mine = jnp.logical_and(own[...] == gy + 64 * slot, q48 // 16 == src)
    slot_block = jnp.sum(jnp.where(mine, blk[...] + 1, 0), axis=1, keepdims=True) - 1
    column = lax.shift_right_arithmetic(slot_block, 3)
    hot = jnp.where(column == lax.broadcasted_iota(jnp.int32, (48, 256), 1), 1.0, 0.0)
    hot = jnp.transpose(jnp.concatenate([hot, jnp.zeros((80, 256), F32)], axis=0)).astype(BF16)
    hot_early = jnp.concatenate([hot[:, :32], hot[:, :32]], axis=1)
    hot_late = jnp.concatenate([hot[:, 32:48], hot[:, 32:48]], axis=1)

    loads[6].wait()

    def turned_rows(first, count, at):
        out = []
        for s in range(2):
            zb = jnp.bitwise_and(slot_block[at + count * s : at + count * (s + 1)], 7)
            for c in range(3):
                row = mrecv[first : first + count, c, :]
                for b in range(3):
                    row = jnp.where(jnp.bitwise_and(zb, 1 << b) > 0, pltpu.roll(row, 16 << b, 1), row)
                out.append((s, c, zb, row))
        return out

    def placed(rows, count, hot, n):
        lanes = lax.broadcasted_iota(jnp.int32, (count, 128), 1) // 16
        parts = [[], []]
        for s, c, zb, row in rows:
            shift = (-16 * (4 * s + n)) % 128
            moved = pltpu.roll(row, shift, 1) if shift else row
            parts[s].append(jnp.where(lanes == zb, moved, 0.0))
        w = jnp.concatenate([jnp.concatenate(part, axis=1) for part in parts], axis=0)
        return jnp.dot(hot, two_parts(w), preferred_element_type=F32)

    def stencil(step, c, x, halo, lo=16, rows=16):
        here = pl.ds(lo, rows)
        v = U[step, c, x + 2, here]
        lanes = lax.broadcasted_iota(jnp.int32, (rows, 128), 1)
        z = (
            jnp.where(lanes == 0, 0.0, pltpu.roll(v, 1, 1))
            + jnp.where(lanes == 127, 0.0, pltpu.roll(v, 127, 1))
            + jnp.where(lanes == edge, halo, 0.0)
        )
        y = U[step, c, x + 2, pl.ds(lo - 1, rows)] + U[step, c, x + 2, pl.ds(lo + 1, rows)]
        around = (U[step, c, x + 1, here] + U[step, c, x + 3, here]) + y + z
        old = up[c, x] if step == 0 else U[step - 1, c, x + 2, here]
        return (2.0 * v - old) + rate[x + 1, here] * (around - 6.0 * v)

    def to_edge(packed, place):
        return pltpu.roll(packed, 128 - place, 1) if place else packed

    order = [0, 15, 1, 14] + list(range(2, 14))

    def received(packed):
        return pltpu.roll(packed, jnp.bitwise_and(127 + 2 * gz, 127), 1)

    def answer(came, reply):
        arrive(came)
        start(reply)

    pl.when(jnp.logical_not(lead_z))(lambda: answer(across, across))
    answer(down, up_gy)
    pl.when(jnp.logical_not(lead_right))(lambda: answer(left, right))
    pl.when(gx == middle)(lambda: answer(right, left))

    def message_wait(peer):
        message_copy(peer, peer).wait_recv()

    def message_reply(peer):
        message_copy(peer, peer).wait_recv()
        message_copy(peer, gy).start()

    answered = jnp.where(jnp.logical_and(gx == 0, gy == 0), 16, gy + 1)
    pl.loop(gy + 1, answered)(message_reply)
    pl.when(lead_z)(lambda: arrive(across))
    arrive(up_gy)
    pl.when(lead_right)(lambda: arrive(left))
    pl.when(gx != middle)(lambda: arrive(right))
    sides = [(-1, 0, 0), (1, 0, 0), (0, -1, 0), (0, 1, 0)]
    beside_count = 0
    for to in sides:
        there = exists(to[0], to[1])
        beside_count = beside_count + there.astype(jnp.int32)
        pl.when(there)(
            lambda to=to: pl.semaphore_signal(known, inc=1, device_id=device(*to), device_id_type=MESH)
        )
    rate[0:1, 16:32] = lat[0:1, 16:32] * speed[None]
    rate[17:18, 16:32] = lat[17:18, 16:32] * speed[None]
    rate[1:17, 8:16] = lat[1:17, 8:16] * speed[None]
    rate[1:17, 32:40] = lat[1:17, 32:40] * speed[None]
    halo0 = received(zrecv[0])
    for x in order:
        for c in range(3):
            U[1, c, x + 2, 16:32] = stencil(0, c, x, to_edge(halo0, 16 * c + x))

    turn = jnp.where(gy < 8, 16, n_gy)
    pl.loop(answered, turn)(message_reply)
    pl.loop(0, jnp.minimum(gy, 16))(message_wait)
    rows = turned_rows(0, 16, 0)
    D[0] = placed(rows, 16, hot_early, 0)
    D1[:, 16:32] = placed(rows, 16, hot_early, 1).reshape(16, 16, 384)
    for n in (2, 3):
        D[n - 1] = placed(rows, 16, hot_early, n)
    pl.loop(turn, n_gy)(message_reply)
    pl.loop(16, gy)(message_wait)
    rows = turned_rows(16, 8, 32)
    drive = D[0] + placed(rows, 8, hot_late, 0)
    D1[:, 16:32] = D1[:, 16:32] + placed(rows, 8, hot_late, 1).reshape(16, 16, 384)
    edge_1 = inner_1 = edge_d = jnp.zeros((16, 128), F32)
    inward = jnp.where(gz == 0, 1, 127)
    for x in order:
        for c in range(3):
            new = U[1, c, x + 2, 16:32] + drive[16 * x : 16 * x + 16, 128 * c : 128 * c + 128]
            U[1, c, x + 2, 16:32] = new
            edge_1 = pack(16 * c + x, new, edge_1)
            inner_1 = pack(16 * c + x, pltpu.roll(new, inward, 1), inner_1)
            edge_d = pack(16 * c + x, D1[x, 16:32, 128 * c : 128 * c + 128], edge_d)
        if x == 14:
            start(deep_x)
    zsend[2] = edge_1
    zsend[3] = inner_1
    zsend[4] = edge_d
    pl.semaphore_wait(known, beside_count)
    start(deep_y)
    start(deep_z)
    for n in (2, 3):
        D[n - 1] = D[n - 1] + placed(rows, 8, hot_late, n)

    arrive(deep_z)
    arrive(deep_y)
    arrive(deep_x)
    halo1 = received(zrecv[2])
    left1, right1 = received(zside[0]), received(zside[1])
    tall = received(jnp.concatenate([zrow[0], zrecv[2], zrow[1]], axis=0))[4:28]
    for c in range(3):
        U[2, c, 1, 16:32] = stencil(1, c, -1, to_edge(left1, 16 * c + 15)) + D1x[0, :, 128 * c : 128 * c + 128]
        U[2, c, 18, 16:32] = stencil(1, c, 16, to_edge(right1, 16 * c)) + D1x[1, :, 128 * c : 128 * c + 128]
        for x in range(16):
            U[2, c, x + 2, 12:36] = (
                stencil(1, c, x, to_edge(tall, 16 * c + x), 12, 24) + D1[x, 12:36, 128 * c : 128 * c + 128]
            )
    x_of = jnp.bitwise_and(lane16 - edge, 15)
    row16 = lax.broadcasted_iota(jnp.int32, (16, 128), 0)
    beside = (
        jnp.where(x_of == 0, pltpu.roll(left1, 113, 1), pltpu.roll(halo1, 1, 1))
        + jnp.where(x_of == 15, pltpu.roll(right1, 15, 1), pltpu.roll(halo1, 127, 1))
        + tall[3:19] + tall[5:21] + edge_1 + received(zrecv[3])
    )
    halo = (2.0 * halo1 - halo0) + received(zrecv[1]) * (beside - 6.0 * halo1) + received(zrecv[4])

    packed = jnp.zeros((16, 128), F32)
    for x in order:
        for c in range(3):
            drive = D[1, 16 * x : 16 * x + 16, 128 * c : 128 * c + 128]
            new = stencil(2, c, x, to_edge(halo, 16 * c + x)) + drive
            U[3, c, x + 2, 16:32] = new
            packed = pack(16 * c + x, new, packed)
            out_prev[c, x] = new
        if x == 15:
            start(last_x)
    zsend[5] = packed
    start(last_yz)

    arrive(last_yz)
    arrive(last_x)
    halo = received(zrecv[5])
    for x in order:
        for c in range(3):
            drive = D[2, 16 * x : 16 * x + 16, 128 * c : 128 * c + 128]
            out_now[c, x] = stencil(3, c, x, to_edge(halo, 16 * c + x)) + drive

    for copies in (left, right, down, up_gy, across, deep_x, deep_y, deep_z, last_x, last_yz):
        sent(copies)

    @pl.loop(1, n_gy)
    def _(k):
        message_copy(lax.rem(gy + k, n_gy), gy).wait_send()


def per_device(n_gx, n_gy, u_now, u_prev, panels, panel_owner, panel_block, coupling, layer_depth, layer_speed, lateral):
    spectral = panels.shape[4]
    count = panel_owner.shape[2]
    layers = layer_speed.shape[0]
    table = jnp.asarray(wave_table(spectral))
    anywhere = pl.BlockSpec(memory_space=pl.ANY)
    vmem = pl.BlockSpec(memory_space=pltpu.VMEM)
    dma = pltpu.SemaphoreType.DMA
    return pl.pallas_call(
        functools.partial(kernel, n_gx, n_gy),
        out_shape=(pltpu.VMEM(u_now.shape, F32), pltpu.VMEM(u_now.shape, F32)),
        in_specs=[anywhere] * 10,
        out_specs=(vmem, vmem),
        scratch_shapes=[
            pltpu.VMEM((NSTEP, 3, 20, 48, 128), F32),
            pltpu.VMEM(u_prev.shape, F32),
            pltpu.VMEM((768, spectral), BF16),
            pltpu.VMEM((1, count), jnp.int32),
            pltpu.VMEM((1, count), jnp.int32),
            pltpu.VMEM(coupling.shape, F32),
            pltpu.VMEM((1, 128), jnp.int32),
            pltpu.VMEM((1, layers), F32),
            pltpu.VMEM((18, 48, 128), F32),
            pltpu.VMEM(table.shape, BF16),
            pltpu.VMEM((8, 16, 128), F32),
            pltpu.VMEM((3, 256, 384), F32),
            pltpu.VMEM((24, 3, 128), F32),
            pltpu.VMEM((24, 3, 128), F32),
            pltpu.VMEM((18, 48, 128), F32),
            pltpu.VMEM((16, 48, 384), F32),
            pltpu.VMEM((2, 16, 384), F32),
            pltpu.VMEM((6, 16, 128), F32),
            pltpu.VMEM((6, 16, 128), F32),
            pltpu.VMEM((2, 16, 128), F32),
            pltpu.VMEM((2, 8, 128), F32),
            dma((10,)),
            dma((24,)),
            dma((24,)),
            dma((31,)),
            dma((31,)),
            pltpu.SemaphoreType.REGULAR,
        ],
        compiler_params=pltpu.CompilerParams(collective_id=0, has_side_effects=True),
        name="domain_reduction",
    )(
        u_now, u_prev, panels.reshape(768, spectral), panel_owner.reshape(1, count), panel_block.reshape(1, count),
        coupling, layer_depth.reshape(1, 128), layer_speed.reshape(1, layers), lateral, table,
    )


def solution(mesh):
    in_specs = (
        P(None, "gx", "gy", "gz"),
        P(None, "gx", "gy", "gz"),
        P("gx", "gz", "gy", None, None),
        P("gx", "gz", None, None),
        P("gx", "gz", None),
        P(),
        P("gz"),
        P(),
        P("gx", "gy", "gz"),
    )
    out_specs = (P(None, "gx", "gy", "gz"), P(None, "gx", "gy", "gz"))
    return jax.shard_map(
        functools.partial(per_device, mesh.shape["gx"], mesh.shape["gy"]),
        mesh=mesh, in_specs=in_specs, out_specs=out_specs, check_vma=False,
    )
```

```python
import functools

import jax
import jax.numpy as jnp
import ml_dtypes
import numpy as np
from jax import lax
from jax.experimental import pallas as pl
from jax.experimental.pallas import tpu as pltpu
from jax.sharding import PartitionSpec as P

NSTEP = 4
MESH = pl.DeviceIdType.MESH
F32 = jnp.float32
BF16 = jnp.bfloat16


def wave_table(count):
    half = count // 2
    freq = np.float32(2.0 * np.pi) * (np.arange(half, dtype=np.float32) + np.float32(0.5)) / np.float32(count)
    times = np.float32(37.0) + np.arange(NSTEP, dtype=np.float32)
    phase = (freq[:, None] * times[None, :]).astype(np.float32)
    table = np.concatenate([np.cos(phase), np.sin(phase)], axis=0) / np.sqrt(np.float32(half))
    table = np.pad(table.T, ((0, 8 - NSTEP), (0, 0)))
    return table.astype(ml_dtypes.bfloat16)


def two_parts(b):
    hi = b.astype(BF16)
    lo = (b - hi.astype(F32)).astype(BF16)
    return jnp.concatenate([hi, lo], axis=0)


def kernel(
    n_gx, n_gy, u_hbm, up_hbm, pan_hbm, own_hbm, blk_hbm, cpl_hbm, dep_hbm, spd_hbm, lat_hbm, tab_hbm,
    out_now, out_prev,
    U, up, pan, own, blk, cpl, dep, spd, lat, tab, G, D, msend, mrecv,
    rate, D1, D1x, zsend, zrecv, zside, zrow, in_sem, fsend_sem, frecv_sem, send_sem, recv_sem, known,
):
    gx, gy, gz = lax.axis_index("gx"), lax.axis_index("gy"), lax.axis_index("gz")
    loads = [
        pltpu.make_async_copy(pan_hbm, pan, in_sem.at[0]),
        pltpu.make_async_copy(tab_hbm, tab, in_sem.at[1]),
        pltpu.make_async_copy(own_hbm, own, in_sem.at[2]),
        pltpu.make_async_copy(blk_hbm, blk, in_sem.at[3]),
        pltpu.make_async_copy(cpl_hbm, cpl, in_sem.at[4]),
        pltpu.make_async_copy(u_hbm, U.at[0, :, 2:18, 16:32], in_sem.at[5]),
        pltpu.make_async_copy(up_hbm, up, in_sem.at[6]),
        pltpu.make_async_copy(lat_hbm, lat.at[1:17, 16:32], in_sem.at[7]),
        pltpu.make_async_copy(dep_hbm, dep, in_sem.at[8]),
        pltpu.make_async_copy(spd_hbm, spd, in_sem.at[9]),
    ]
    for at in (2, 0, 1, 3, 4, 5, 6, 7, 8, 9):
        loads[at].start()

    barrier = pltpu.get_barrier_semaphore()

    has_left, has_right = gx > 0, gx < n_gx - 1
    has_down, has_up = gy > 0, gy < n_gy - 1

    def exists(dx, dy):
        there = gx >= 0
        if dx:
            there = has_right if dx > 0 else has_left
        if dy:
            there = jnp.logical_and(there, has_up if dy > 0 else has_down)
        return there

    def device(dx, dy, dz):
        return {"gx": gx + dx, "gy": gy + dy, "gz": 1 - gz if dz else gz}

    middle = n_gx // 2
    lead_left = jnp.logical_and(has_left, gx != middle)
    lead_right = gx == middle - 1
    lead_z = gz == 1
    told_right = jnp.logical_and(has_right, gx != middle - 1)

    def tell(there, to):
        pl.when(there)(
            lambda: pl.semaphore_signal(barrier, inc=1, device_id=device(*to), device_id_type=MESH)
        )

    tell(gx == middle, (-1, 0, 0))
    tell(told_right, (1, 0, 0))
    lonely = jnp.logical_and(gy == 0, jnp.logical_or(gx == 0, gx == middle))
    tell(jnp.logical_or(gz == 0, lonely), (0, 0, 1))
    told_z = jnp.logical_or(lead_z, lonely)
    count = gy + lead_left.astype(jnp.int32) + lead_right.astype(jnp.int32) + told_z.astype(jnp.int32)

    @pl.loop(gy + 1, n_gy)
    def _(peer):
        pl.semaphore_signal(barrier, inc=1, device_id={"gy": peer}, device_id_type=MESH)

    @pl.when(jnp.logical_not(has_left))
    def _():
        U[:, :, 0:2, 8:40] = jnp.zeros((NSTEP, 3, 2, 32, 128), F32)
        lat[0, 16:32] = jnp.zeros((16, 128), F32)
        D1x[0] = jnp.zeros((16, 384), F32)
        zside[0] = jnp.zeros((16, 128), F32)

    @pl.when(jnp.logical_not(has_right))
    def _():
        U[:, :, 18:20, 8:40] = jnp.zeros((NSTEP, 3, 2, 32, 128), F32)
        lat[17, 16:32] = jnp.zeros((16, 128), F32)
        D1x[1] = jnp.zeros((16, 384), F32)
        zside[1] = jnp.zeros((16, 128), F32)

    @pl.when(jnp.logical_not(has_down))
    def _():
        U[:, :, :, 8:16] = jnp.zeros((NSTEP, 3, 20, 8, 128), F32)
        lat[1:17, 8:16] = jnp.zeros((16, 8, 128), F32)
        D1[:, 8:16] = jnp.zeros((16, 8, 384), F32)
        zrow[0] = jnp.zeros((8, 128), F32)

    @pl.when(jnp.logical_not(has_up))
    def _():
        U[:, :, :, 32:40] = jnp.zeros((NSTEP, 3, 20, 8, 128), F32)
        lat[1:17, 32:40] = jnp.zeros((16, 8, 128), F32)
        D1[:, 32:40] = jnp.zeros((16, 8, 384), F32)
        zrow[1] = jnp.zeros((8, 128), F32)

    edge = 127 - 127 * gz
    lane16 = lax.broadcasted_iota(jnp.int32, (16, 128), 1)

    loads[2].wait()
    owner = own[...]
    q = lax.broadcasted_iota(jnp.int32, (1, 384), 1)
    rank = jnp.zeros((1, 384), jnp.int32)
    for d in range(1, 16):
        same = jnp.logical_and(q % 16 >= d, pltpu.roll(owner, d, 1) == owner)
        rank = rank + same.astype(jnp.int32)
    own[...] = owner + 64 * rank

    tile = gy // 8
    off = (gy - 8 * tile) * 16
    lane1 = lax.broadcasted_iota(jnp.int32, (1, 128), 1)
    mycode = own[:, pl.ds(pl.multiple_of(tile * 128, 128), 128)]
    mycode = jnp.where(jnp.logical_and(lane1 >= off, lane1 < off + 16), mycode, 0)
    for s in (16, 32, 64):
        mycode = mycode + pltpu.roll(mycode, s, 1)
    r192 = lax.broadcasted_iota(jnp.int32, (192, 128), 0)
    l192 = lax.broadcasted_iota(jnp.int32, (192, 128), 1)
    want = (r192 % 24) + 64 * (r192 // 96)
    step_of = (r192 // 24) % 4
    pick = jnp.where(jnp.logical_and(mycode == want, l192 // 16 == step_of), 1.0, 0.0).astype(BF16)
    pick = jnp.concatenate([pick, pick], axis=1)

    G[...] = jnp.zeros_like(G)
    loads[4].wait()
    zero = jnp.zeros((16, 16), F32)
    stiff = jnp.concatenate(
        [jnp.concatenate([cpl[c] if c == k else zero for k in range(3)], axis=1) for c in range(3)], axis=0
    )
    loads[0].wait()
    loads[1].wait()
    free = lax.dot_general(tab[...], pan[...], (((1,), (1,)), ((), ())), preferred_element_type=F32)
    for p in range(16):
        G[:, p, :48] = free[:, 48 * p : 48 * p + 48]
    force = lax.dot_general(
        G[...].reshape(128, 128)[:, :48], stiff, (((1,), (1,)), ((), ())),
        precision=lax.Precision.HIGHEST, preferred_element_type=F32,
    )
    picked = jnp.dot(pick, two_parts(force), preferred_element_type=F32)
    picked = jnp.concatenate([picked, jnp.zeros((192, 80), F32)], axis=1)
    lane24 = lax.broadcasted_iota(jnp.int32, (24, 128), 1)
    for c in range(3):
        message = jnp.zeros((24, 128), F32)
        for sn in range(8):
            part = picked[24 * sn : 24 * sn + 24]
            shift = (16 * (sn - c)) % 128
            if shift:
                part = pltpu.roll(part, shift, 1)
            message = jnp.where(lane24 // 16 == sn, part, message)
        msend[:, c, :] = message
    mrecv[gy] = msend[gy]

    loads[5].wait()
    loads[7].wait()
    pl.semaphore_wait(barrier, count)

    def message_copy(peer, sender):
        return pltpu.make_async_remote_copy(
            src_ref=msend.at[peer], dst_ref=mrecv.at[sender], send_sem=fsend_sem.at[peer],
            recv_sem=frecv_sem.at[sender], device_id={"gy": peer}, device_id_type=MESH,
        )

    def exchange(first, moves):
        return [
            (
                to,
                pltpu.make_async_remote_copy(
                    src_ref=src, dst_ref=dst, send_sem=send_sem.at[first + k], recv_sem=recv_sem.at[first + k],
                    device_id=device(*to), device_id_type=MESH,
                ),
            )
            for k, (to, src, dst) in enumerate(moves)
        ]

    def start(copies):
        for to, copy in copies:
            pl.when(exists(to[0], to[1]))(copy.start)

    def arrive(copies):
        for to, copy in copies:
            pl.when(exists(-to[0], -to[1]))(copy.wait_recv)

    def sent(copies):
        for to, copy in copies:
            pl.when(exists(to[0], to[1]))(copy.wait_send)

    def x_faces(step, width):
        return [
            ((-1, 0, 0), U.at[step, :, 2 : 2 + width, 16:32], U.at[step, :, 18 : 18 + width, 16:32]),
            ((1, 0, 0), U.at[step, :, 18 - width : 18, 16:32], U.at[step, :, 2 - width : 2, 16:32]),
        ]

    def y_faces(step, width):
        return [
            ((0, -1, 0), U.at[step, :, 2:18, 16 : 16 + width], U.at[step, :, 2:18, 32 : 32 + width]),
            ((0, 1, 0), U.at[step, :, 2:18, 32 - width : 32], U.at[step, :, 2:18, 16 - width : 16]),
        ]

    (u_left, u_right), (u_down, u_up) = x_faces(0, 1), y_faces(0, 1)
    left = exchange(0, [u_left, ((-1, 0, 0), lat.at[1, 16:32], lat.at[17, 16:32])])
    right = exchange(2, [u_right, ((1, 0, 0), lat.at[16, 16:32], lat.at[0, 16:32])])
    down = exchange(4, [u_down, ((0, -1, 0), lat.at[1:17, 16:17], lat.at[1:17, 32:33])])
    up_gy = exchange(6, [u_up, ((0, 1, 0), lat.at[1:17, 31:32], lat.at[1:17, 15:16])])
    across = exchange(8, [((0, 0, 1), zsend.at[0:2], zrecv.at[0:2])])
    deep_x = exchange(9, x_faces(1, 2) + [
        ((-1, 0, 0), D1.at[0, 16:32], D1x.at[1]),
        ((1, 0, 0), D1.at[15, 16:32], D1x.at[0]),
    ])
    corners = exchange(13, [
        ((dx, dy, 0), U.at[1, :, 2 if dx < 0 else 17, pl.ds(16 if dy < 0 else 31, 1)],
         U.at[1, :, 18 if dx < 0 else 1, pl.ds(32 if dy < 0 else 15, 1)])
        for dx in (-1, 1) for dy in (-1, 1)
    ])
    deep_y = exchange(17, y_faces(1, 2) + [
        ((0, -1, 0), D1.at[:, 16:17], D1.at[:, 32:33]),
        ((0, 1, 0), D1.at[:, 31:32], D1.at[:, 15:16]),
    ])
    deep_xz = exchange(21, [
        ((-1, 0, 1), zsend.at[2], zside.at[1]),
        ((1, 0, 1), zsend.at[2], zside.at[0]),
    ])
    deep_z = exchange(23, [
        ((0, -1, 1), zsend.at[2, 0:8], zrow.at[1]),
        ((0, 1, 1), zsend.at[2, 8:16], zrow.at[0]),
        ((0, 0, 1), zsend.at[2:5], zrecv.at[2:5]),
    ])
    last_x = exchange(26, x_faces(3, 1))
    last_yz = exchange(28, y_faces(3, 1) + [((0, 0, 1), zsend.at[5], zrecv.at[5])])

    def pack(place, value, packed):
        turned = pltpu.roll(value, place, 1) if place else value
        return jnp.where(lane16 == jnp.bitwise_and(edge + place, 127), turned, packed)

    @pl.loop(0, gy)
    def _(peer):
        message_copy(peer, gy).start()

    pl.when(lead_left)(lambda: start(left))
    pl.when(lead_right)(lambda: start(right))
    start(down)

    for copy in (loads[8], loads[9]):
        copy.wait()
    speed = jnp.zeros((1, 128), F32)
    for layer in range(spd.shape[1]):
        speed = jnp.where(dep[...] == layer, spd[0:1, layer : layer + 1], speed)
    rate[1:17, 16:32] = lat[1:17, 16:32] * speed[None]
    packed, packed_rate = jnp.zeros((16, 128), F32), jnp.zeros((16, 128), F32)
    for c in range(3):
        for x in range(16):
            packed = pack(16 * c + x, U[0, c, x + 2, 16:32], packed)
            packed_rate = pack(16 * c + x, rate[x + 1, 16:32], packed_rate)
    zsend[0] = packed
    zsend[1] = packed_rate
    pl.when(lead_z)(lambda: start(across))

    loads[3].wait()
    k48 = lax.broadcasted_iota(jnp.int32, (48, 384), 0)
    q48 = lax.broadcasted_iota(jnp.int32, (48, 384), 1)
    late = k48 >= 32
    slot = jnp.where(late, (k48 - 32) // 8, k48 // 16)
    src = jnp.where(late, 16 + k48 % 8, k48 % 16)
    mine = jnp.logical_and(own[...] == gy + 64 * slot, q48 // 16 == src)
    slot_block = jnp.sum(jnp.where(mine, blk[...] + 1, 0), axis=1, keepdims=True) - 1
    column = lax.shift_right_arithmetic(slot_block, 3)
    hot = jnp.where(column == lax.broadcasted_iota(jnp.int32, (48, 256), 1), 1.0, 0.0)
    hot = jnp.transpose(jnp.concatenate([hot, jnp.zeros((80, 256), F32)], axis=0)).astype(BF16)
    hot_early = jnp.concatenate([hot[:, :32], hot[:, :32]], axis=1)
    hot_late = jnp.concatenate([hot[:, 32:48], hot[:, 32:48]], axis=1)

    loads[6].wait()

    def turned_rows(first, count, at):
        out = []
        for s in range(2):
            zb = jnp.bitwise_and(slot_block[at + count * s : at + count * (s + 1)], 7)
            for c in range(3):
                row = mrecv[first : first + count, c, :]
                for b in range(3):
                    row = jnp.where(jnp.bitwise_and(zb, 1 << b) > 0, pltpu.roll(row, 16 << b, 1), row)
                out.append((s, c, zb, row))
        return out

    def placed(rows, count, hot, n):
        lanes = lax.broadcasted_iota(jnp.int32, (count, 128), 1) // 16
        parts = [[], []]
        for s, c, zb, row in rows:
            shift = (-16 * (4 * s + n)) % 128
            moved = pltpu.roll(row, shift, 1) if shift else row
            parts[s].append(jnp.where(lanes == zb, moved, 0.0))
        w = jnp.concatenate([jnp.concatenate(part, axis=1) for part in parts], axis=0)
        return jnp.dot(hot, two_parts(w), preferred_element_type=F32)

    def stencil(step, c, x, halo, lo=16, rows=16):
        here = pl.ds(lo, rows)
        v = U[step, c, x + 2, here]
        lanes = lax.broadcasted_iota(jnp.int32, (rows, 128), 1)
        z = (
            jnp.where(lanes == 0, 0.0, pltpu.roll(v, 1, 1))
            + jnp.where(lanes == 127, 0.0, pltpu.roll(v, 127, 1))
            + jnp.where(lanes == edge, halo, 0.0)
        )
        y = U[step, c, x + 2, pl.ds(lo - 1, rows)] + U[step, c, x + 2, pl.ds(lo + 1, rows)]
        around = (U[step, c, x + 1, here] + U[step, c, x + 3, here]) + y + z
        old = up[c, x] if step == 0 else U[step - 1, c, x + 2, here]
        return (2.0 * v - old) + rate[x + 1, here] * (around - 6.0 * v)

    def to_edge(packed, place):
        return pltpu.roll(packed, 128 - place, 1) if place else packed

    order = [0, 15, 1, 14] + list(range(2, 14))

    def received(packed):
        return pltpu.roll(packed, jnp.bitwise_and(127 + 2 * gz, 127), 1)

    def answer(came, reply):
        arrive(came)
        start(reply)

    pl.when(jnp.logical_not(lead_z))(lambda: answer(across, across))
    answer(down, up_gy)
    pl.when(jnp.logical_not(lead_right))(lambda: answer(left, right))
    pl.when(gx == middle)(lambda: answer(right, left))

    def message_wait(peer):
        message_copy(peer, peer).wait_recv()

    def message_reply(peer):
        message_copy(peer, peer).wait_recv()
        message_copy(peer, gy).start()

    answered = jnp.where(jnp.logical_and(gx == 0, gy == 0), 16, gy + 1)
    pl.loop(gy + 1, answered)(message_reply)
    pl.when(lead_z)(lambda: arrive(across))
    arrive(up_gy)
    pl.when(lead_right)(lambda: arrive(left))
    pl.when(gx != middle)(lambda: arrive(right))
    sides = [(-1, 0, 0), (1, 0, 0), (0, -1, 0), (0, 1, 0)]
    beside_count = 0
    for to in sides:
        there = exists(to[0], to[1])
        beside_count = beside_count + there.astype(jnp.int32)
        pl.when(there)(
            lambda to=to: pl.semaphore_signal(known, inc=1, device_id=device(*to), device_id_type=MESH)
        )
    rate[0:1, 16:32] = lat[0:1, 16:32] * speed[None]
    rate[17:18, 16:32] = lat[17:18, 16:32] * speed[None]
    rate[1:17, 8:16] = lat[1:17, 8:16] * speed[None]
    rate[1:17, 32:40] = lat[1:17, 32:40] * speed[None]
    halo0 = received(zrecv[0])
    for x in order:
        for c in range(3):
            U[1, c, x + 2, 16:32] = stencil(0, c, x, to_edge(halo0, 16 * c + x))

    turn = jnp.where(gy < 8, 16, n_gy)
    pl.loop(answered, turn)(message_reply)
    pl.loop(0, jnp.minimum(gy, 16))(message_wait)
    rows = turned_rows(0, 16, 0)
    D[0] = placed(rows, 16, hot_early, 0)
    D1[:, 16:32] = placed(rows, 16, hot_early, 1).reshape(16, 16, 384)
    for n in (2, 3):
        D[n - 1] = placed(rows, 16, hot_early, n)
    pl.loop(turn, n_gy)(message_reply)
    pl.loop(16, gy)(message_wait)
    rows = turned_rows(16, 8, 32)
    drive = D[0] + placed(rows, 8, hot_late, 0)
    D1[:, 16:32] = D1[:, 16:32] + placed(rows, 8, hot_late, 1).reshape(16, 16, 384)
    edge_1 = inner_1 = edge_d = jnp.zeros((16, 128), F32)
    inward = jnp.where(gz == 0, 1, 127)
    for x in order:
        for c in range(3):
            new = U[1, c, x + 2, 16:32] + drive[16 * x : 16 * x + 16, 128 * c : 128 * c + 128]
            U[1, c, x + 2, 16:32] = new
            edge_1 = pack(16 * c + x, new, edge_1)
            inner_1 = pack(16 * c + x, pltpu.roll(new, inward, 1), inner_1)
            edge_d = pack(16 * c + x, D1[x, 16:32, 128 * c : 128 * c + 128], edge_d)
        if x == 14:
            start(deep_x)
    zsend[2] = edge_1
    zsend[3] = inner_1
    zsend[4] = edge_d
    pl.semaphore_wait(known, beside_count)
    start(corners)
    start(deep_xz)
    start(deep_y)
    start(deep_z)
    for n in (2, 3):
        D[n - 1] = D[n - 1] + placed(rows, 8, hot_late, n)

    arrive(deep_z)
    arrive(deep_y)
    halo1 = received(zrecv[2])
    tall = received(jnp.concatenate([zrow[0], zrecv[2], zrow[1]], axis=0))[4:28]

    def second(x):
        for c in range(3):
            U[2, c, x + 2, 12:36] = (
                stencil(1, c, x, to_edge(tall, 16 * c + x), 12, 24) + D1[x, 12:36, 128 * c : 128 * c + 128]
            )

    for x in range(1, 15):
        second(x)
    arrive(corners)
    arrive(deep_xz)
    arrive(deep_x)
    left1, right1 = received(zside[0]), received(zside[1])
    for c in range(3):
        U[2, c, 1, 16:32] = stencil(1, c, -1, to_edge(left1, 16 * c + 15)) + D1x[0, :, 128 * c : 128 * c + 128]
        U[2, c, 18, 16:32] = stencil(1, c, 16, to_edge(right1, 16 * c)) + D1x[1, :, 128 * c : 128 * c + 128]
    second(0)
    second(15)
    x_of = jnp.bitwise_and(lane16 - edge, 15)
    beside = (
        jnp.where(x_of == 0, pltpu.roll(left1, 113, 1), pltpu.roll(halo1, 1, 1))
        + jnp.where(x_of == 15, pltpu.roll(right1, 15, 1), pltpu.roll(halo1, 127, 1))
        + tall[3:19] + tall[5:21] + edge_1 + received(zrecv[3])
    )
    halo = (2.0 * halo1 - halo0) + received(zrecv[1]) * (beside - 6.0 * halo1) + received(zrecv[4])

    packed = jnp.zeros((16, 128), F32)
    for x in order:
        for c in range(3):
            drive = D[1, 16 * x : 16 * x + 16, 128 * c : 128 * c + 128]
            new = stencil(2, c, x, to_edge(halo, 16 * c + x)) + drive
            U[3, c, x + 2, 16:32] = new
            packed = pack(16 * c + x, new, packed)
            out_prev[c, x] = new
        if x == 15:
            start(last_x)
    zsend[5] = packed
    start(last_yz)

    arrive(last_yz)
    halo = received(zrecv[5])

    def last(x):
        for c in range(3):
            drive = D[2, 16 * x : 16 * x + 16, 128 * c : 128 * c + 128]
            out_now[c, x] = stencil(3, c, x, to_edge(halo, 16 * c + x)) + drive

    for x in range(1, 15):
        last(x)
    arrive(last_x)
    last(0)
    last(15)

    for copies in (left, right, down, up_gy, across, deep_x, corners, deep_y, deep_xz, deep_z, last_x, last_yz):
        sent(copies)

    @pl.loop(1, n_gy)
    def _(k):
        message_copy(lax.rem(gy + k, n_gy), gy).wait_send()


def write_out(now_in, prev_in, now_out, prev_out, sem):
    copies = [pltpu.make_async_copy(now_in, now_out, sem.at[0]), pltpu.make_async_copy(prev_in, prev_out, sem.at[1])]
    for copy in copies:
        copy.start()
    for copy in copies:
        copy.wait()


def per_device(n_gx, n_gy, u_now, u_prev, panels, panel_owner, panel_block, coupling, layer_depth, layer_speed, lateral):
    spectral = panels.shape[4]
    count = panel_owner.shape[2]
    layers = layer_speed.shape[0]
    table = jnp.asarray(wave_table(spectral))
    anywhere = pl.BlockSpec(memory_space=pl.ANY)
    vmem = pl.BlockSpec(memory_space=pltpu.VMEM)
    dma = pltpu.SemaphoreType.DMA
    now, prev = pl.pallas_call(
        functools.partial(kernel, n_gx, n_gy),
        out_shape=(pltpu.VMEM(u_now.shape, F32), pltpu.VMEM(u_now.shape, F32)),
        in_specs=[anywhere] * 10,
        out_specs=(vmem, vmem),
        scratch_shapes=[
            pltpu.VMEM((NSTEP, 3, 20, 48, 128), F32),
            pltpu.VMEM(u_prev.shape, F32),
            pltpu.VMEM((768, spectral), BF16),
            pltpu.VMEM((1, count), jnp.int32),
            pltpu.VMEM((1, count), jnp.int32),
            pltpu.VMEM(coupling.shape, F32),
            pltpu.VMEM((1, 128), jnp.int32),
            pltpu.VMEM((1, layers), F32),
            pltpu.VMEM((18, 48, 128), F32),
            pltpu.VMEM(table.shape, BF16),
            pltpu.VMEM((8, 16, 128), F32),
            pltpu.VMEM((3, 256, 384), F32),
            pltpu.VMEM((24, 3, 128), F32),
            pltpu.VMEM((24, 3, 128), F32),
            pltpu.VMEM((18, 48, 128), F32),
            pltpu.VMEM((16, 48, 384), F32),
            pltpu.VMEM((2, 16, 384), F32),
            pltpu.VMEM((6, 16, 128), F32),
            pltpu.VMEM((6, 16, 128), F32),
            pltpu.VMEM((2, 16, 128), F32),
            pltpu.VMEM((2, 8, 128), F32),
            dma((10,)),
            dma((24,)),
            dma((24,)),
            dma((31,)),
            dma((31,)),
            pltpu.SemaphoreType.REGULAR,
        ],
        compiler_params=pltpu.CompilerParams(collective_id=0, has_side_effects=True),
        name="domain_reduction",
    )(
        u_now, u_prev, panels.reshape(768, spectral), panel_owner.reshape(1, count), panel_block.reshape(1, count),
        coupling, layer_depth.reshape(1, 128), layer_speed.reshape(1, layers), lateral, table,
    )
    whole = jax.ShapeDtypeStruct(u_now.shape, F32)
    return pl.pallas_call(
        write_out,
        out_shape=(whole, whole),
        in_specs=[vmem, vmem],
        out_specs=(anywhere, anywhere),
        scratch_shapes=[dma((2,))],
        name="write_out",
    )(
        pltpu.with_memory_space_constraint(now, pltpu.VMEM),
        pltpu.with_memory_space_constraint(prev, pltpu.VMEM),
    )


def solution(mesh):
    in_specs = (
        P(None, "gx", "gy", "gz"),
        P(None, "gx", "gy", "gz"),
        P("gx", "gz", "gy", None, None),
        P("gx", "gz", None, None),
        P("gx", "gz", None),
        P(),
        P("gz"),
        P(),
        P("gx", "gy", "gz"),
    )
    out_specs = (P(None, "gx", "gy", "gz"), P(None, "gx", "gy", "gz"))
    return jax.shard_map(
        functools.partial(per_device, mesh.shape["gx"], mesh.shape["gy"]),
        mesh=mesh, in_specs=in_specs, out_specs=out_specs, check_vma=False,
    )
```

```python
import functools

import jax
import jax.numpy as jnp
import ml_dtypes
import numpy as np
from jax import lax
from jax.experimental import pallas as pl
from jax.experimental.pallas import tpu as pltpu
from jax.sharding import PartitionSpec as P

NSTEP = 4
MESH = pl.DeviceIdType.MESH
F32 = jnp.float32
BF16 = jnp.bfloat16


def wave_table(count):
    half = count // 2
    freq = np.float32(2.0 * np.pi) * (np.arange(half, dtype=np.float32) + np.float32(0.5)) / np.float32(count)
    times = np.float32(37.0) + np.arange(NSTEP, dtype=np.float32)
    phase = (freq[:, None] * times[None, :]).astype(np.float32)
    table = np.concatenate([np.cos(phase), np.sin(phase)], axis=0) / np.sqrt(np.float32(half))
    table = np.pad(table.T, ((0, 8 - NSTEP), (0, 0)))
    return table.astype(ml_dtypes.bfloat16)


def two_parts(b):
    hi = b.astype(BF16)
    lo = (b - hi.astype(F32)).astype(BF16)
    return jnp.concatenate([hi, lo], axis=0)


def kernel(
    n_gx, n_gy, u_hbm, up_hbm, pan_hbm, own_hbm, blk_hbm, cpl_hbm, dep_hbm, spd_hbm, lat_hbm, tab_hbm,
    out_now, out_prev,
    U, up, pan, own, blk, cpl, dep, spd, lat, tab, G, D, msend, mrecv,
    rate, D1, D1x, zsend, zrecv, zside, zrow, in_sem, fsend_sem, frecv_sem, send_sem, recv_sem, known,
):
    gx, gy, gz = lax.axis_index("gx"), lax.axis_index("gy"), lax.axis_index("gz")
    loads = [
        pltpu.make_async_copy(pan_hbm, pan, in_sem.at[0]),
        pltpu.make_async_copy(tab_hbm, tab, in_sem.at[1]),
        pltpu.make_async_copy(own_hbm, own, in_sem.at[2]),
        pltpu.make_async_copy(blk_hbm, blk, in_sem.at[3]),
        pltpu.make_async_copy(cpl_hbm, cpl, in_sem.at[4]),
        pltpu.make_async_copy(u_hbm, U.at[0, :, 2:18, 16:32], in_sem.at[5]),
        pltpu.make_async_copy(up_hbm, up, in_sem.at[6]),
        pltpu.make_async_copy(lat_hbm, lat.at[1:17, 16:32], in_sem.at[7]),
        pltpu.make_async_copy(dep_hbm, dep, in_sem.at[8]),
        pltpu.make_async_copy(spd_hbm, spd, in_sem.at[9]),
    ]
    for at in (2, 0, 1, 3, 4, 5, 6, 7, 8, 9):
        loads[at].start()

    barrier = pltpu.get_barrier_semaphore()

    has_left, has_right = gx > 0, gx < n_gx - 1
    has_down, has_up = gy > 0, gy < n_gy - 1

    def exists(dx, dy):
        there = gx >= 0
        if dx:
            there = has_right if dx > 0 else has_left
        if dy:
            there = jnp.logical_and(there, has_up if dy > 0 else has_down)
        return there

    def device(dx, dy, dz):
        return {"gx": gx + dx, "gy": gy + dy, "gz": 1 - gz if dz else gz}

    middle = n_gx // 2
    lead_left = jnp.logical_and(has_left, gx != middle)
    lead_right = gx == middle - 1
    lead_z = gz == 1
    told_right = jnp.logical_and(has_right, gx != middle - 1)

    def tell(there, to):
        pl.when(there)(
            lambda: pl.semaphore_signal(barrier, inc=1, device_id=device(*to), device_id_type=MESH)
        )

    tell(gx == middle, (-1, 0, 0))
    tell(told_right, (1, 0, 0))
    lonely = jnp.logical_and(gy == 0, jnp.logical_or(gx == 0, gx == middle))
    tell(jnp.logical_or(gz == 0, lonely), (0, 0, 1))
    told_z = jnp.logical_or(lead_z, lonely)
    count = gy + lead_left.astype(jnp.int32) + lead_right.astype(jnp.int32) + told_z.astype(jnp.int32)

    @pl.loop(gy + 1, n_gy)
    def _(peer):
        pl.semaphore_signal(barrier, inc=1, device_id={"gy": peer}, device_id_type=MESH)

    @pl.when(jnp.logical_not(has_left))
    def _():
        U[:, :, 0:2, 8:40] = jnp.zeros((NSTEP, 3, 2, 32, 128), F32)
        lat[0, 16:32] = jnp.zeros((16, 128), F32)
        D1x[0] = jnp.zeros((16, 384), F32)
        zside[0] = jnp.zeros((16, 128), F32)

    @pl.when(jnp.logical_not(has_right))
    def _():
        U[:, :, 18:20, 8:40] = jnp.zeros((NSTEP, 3, 2, 32, 128), F32)
        lat[17, 16:32] = jnp.zeros((16, 128), F32)
        D1x[1] = jnp.zeros((16, 384), F32)
        zside[1] = jnp.zeros((16, 128), F32)

    @pl.when(jnp.logical_not(has_down))
    def _():
        U[:, :, :, 8:16] = jnp.zeros((NSTEP, 3, 20, 8, 128), F32)
        lat[1:17, 8:16] = jnp.zeros((16, 8, 128), F32)
        D1[:, 8:16] = jnp.zeros((16, 8, 384), F32)
        zrow[0] = jnp.zeros((8, 128), F32)

    @pl.when(jnp.logical_not(has_up))
    def _():
        U[:, :, :, 32:40] = jnp.zeros((NSTEP, 3, 20, 8, 128), F32)
        lat[1:17, 32:40] = jnp.zeros((16, 8, 128), F32)
        D1[:, 32:40] = jnp.zeros((16, 8, 384), F32)
        zrow[1] = jnp.zeros((8, 128), F32)

    edge = 127 - 127 * gz
    lane16 = lax.broadcasted_iota(jnp.int32, (16, 128), 1)

    loads[2].wait()
    owner = own[...]
    q = lax.broadcasted_iota(jnp.int32, (1, 384), 1)
    rank = jnp.zeros((1, 384), jnp.int32)
    for d in range(1, 16):
        same = jnp.logical_and(q % 16 >= d, pltpu.roll(owner, d, 1) == owner)
        rank = rank + same.astype(jnp.int32)
    own[...] = owner + 64 * rank

    tile = gy // 8
    off = (gy - 8 * tile) * 16
    lane1 = lax.broadcasted_iota(jnp.int32, (1, 128), 1)
    mycode = own[:, pl.ds(pl.multiple_of(tile * 128, 128), 128)]
    mycode = jnp.where(jnp.logical_and(lane1 >= off, lane1 < off + 16), mycode, 0)
    for s in (16, 32, 64):
        mycode = mycode + pltpu.roll(mycode, s, 1)
    r192 = lax.broadcasted_iota(jnp.int32, (192, 128), 0)
    l192 = lax.broadcasted_iota(jnp.int32, (192, 128), 1)
    want = (r192 % 24) + 64 * (r192 // 96)
    step_of = (r192 // 24) % 4
    pick = jnp.where(jnp.logical_and(mycode == want, l192 // 16 == step_of), 1.0, 0.0).astype(BF16)
    pick = jnp.concatenate([pick, pick], axis=1)

    G[...] = jnp.zeros_like(G)
    loads[4].wait()
    zero = jnp.zeros((16, 16), F32)
    stiff = jnp.concatenate(
        [jnp.concatenate([cpl[c] if c == k else zero for k in range(3)], axis=1) for c in range(3)], axis=0
    )
    loads[0].wait()
    loads[1].wait()
    free = lax.dot_general(tab[...], pan[...], (((1,), (1,)), ((), ())), preferred_element_type=F32)
    for p in range(16):
        G[:, p, :48] = free[:, 48 * p : 48 * p + 48]
    force = lax.dot_general(
        G[...].reshape(128, 128)[:, :48], stiff, (((1,), (1,)), ((), ())),
        precision=lax.Precision.HIGHEST, preferred_element_type=F32,
    )
    picked = jnp.dot(pick, two_parts(force), preferred_element_type=F32)
    picked = jnp.concatenate([picked, jnp.zeros((192, 80), F32)], axis=1)
    lane24 = lax.broadcasted_iota(jnp.int32, (24, 128), 1)
    for c in range(3):
        message = jnp.zeros((24, 128), F32)
        for sn in range(8):
            part = picked[24 * sn : 24 * sn + 24]
            shift = (16 * (sn - c)) % 128
            if shift:
                part = pltpu.roll(part, shift, 1)
            message = jnp.where(lane24 // 16 == sn, part, message)
        msend[:, c, :] = message
    mrecv[gy] = msend[gy]

    loads[5].wait()
    loads[7].wait()
    pl.semaphore_wait(barrier, count)

    def message_copy(peer, sender):
        return pltpu.make_async_remote_copy(
            src_ref=msend.at[peer], dst_ref=mrecv.at[sender], send_sem=fsend_sem.at[peer],
            recv_sem=frecv_sem.at[sender], device_id={"gy": peer}, device_id_type=MESH,
        )

    def exchange(first, moves):
        return [
            (
                to,
                pltpu.make_async_remote_copy(
                    src_ref=src, dst_ref=dst, send_sem=send_sem.at[first + k], recv_sem=recv_sem.at[first + k],
                    device_id=device(*to), device_id_type=MESH,
                ),
            )
            for k, (to, src, dst) in enumerate(moves)
        ]

    def start(copies):
        for to, copy in copies:
            pl.when(exists(to[0], to[1]))(copy.start)

    def arrive(copies):
        for to, copy in copies:
            pl.when(exists(-to[0], -to[1]))(copy.wait_recv)

    def sent(copies):
        for to, copy in copies:
            pl.when(exists(to[0], to[1]))(copy.wait_send)

    def x_faces(step, width):
        return [
            ((-1, 0, 0), U.at[step, :, 2 : 2 + width, 16:32], U.at[step, :, 18 : 18 + width, 16:32]),
            ((1, 0, 0), U.at[step, :, 18 - width : 18, 16:32], U.at[step, :, 2 - width : 2, 16:32]),
        ]

    def y_faces(step, width):
        return [
            ((0, -1, 0), U.at[step, :, 2:18, 16 : 16 + width], U.at[step, :, 2:18, 32 : 32 + width]),
            ((0, 1, 0), U.at[step, :, 2:18, 32 - width : 32], U.at[step, :, 2:18, 16 - width : 16]),
        ]

    (u_left, u_right), (u_down, u_up) = x_faces(0, 1), y_faces(0, 1)
    left = exchange(0, [u_left, ((-1, 0, 0), lat.at[1, 16:32], lat.at[17, 16:32])])
    right = exchange(2, [u_right, ((1, 0, 0), lat.at[16, 16:32], lat.at[0, 16:32])])
    down = exchange(4, [u_down, ((0, -1, 0), lat.at[1:17, 16:17], lat.at[1:17, 32:33])])
    up_gy = exchange(6, [u_up, ((0, 1, 0), lat.at[1:17, 31:32], lat.at[1:17, 15:16])])
    across = exchange(8, [((0, 0, 1), zsend.at[0:2], zrecv.at[0:2])])
    deep_x = exchange(9, x_faces(1, 2) + [
        ((-1, 0, 0), D1.at[0, 16:32], D1x.at[1]),
        ((1, 0, 0), D1.at[15, 16:32], D1x.at[0]),
    ])
    corners = exchange(13, [
        ((dx, dy, 0), U.at[1, :, 2 if dx < 0 else 17, pl.ds(16 if dy < 0 else 31, 1)],
         U.at[1, :, 18 if dx < 0 else 1, pl.ds(32 if dy < 0 else 15, 1)])
        for dx in (-1, 1) for dy in (-1, 1)
    ])
    deep_y = exchange(17, y_faces(1, 2) + [
        ((0, -1, 0), D1.at[:, 16:17], D1.at[:, 32:33]),
        ((0, 1, 0), D1.at[:, 31:32], D1.at[:, 15:16]),
    ])
    deep_xz = exchange(21, [
        ((-1, 0, 1), zsend.at[2], zside.at[1]),
        ((1, 0, 1), zsend.at[2], zside.at[0]),
    ])
    deep_z = exchange(23, [
        ((0, -1, 1), zsend.at[2, 0:8], zrow.at[1]),
        ((0, 1, 1), zsend.at[2, 8:16], zrow.at[0]),
        ((0, 0, 1), zsend.at[2:5], zrecv.at[2:5]),
    ])
    last_x = exchange(26, x_faces(3, 1))
    last_yz = exchange(28, y_faces(3, 1) + [((0, 0, 1), zsend.at[5], zrecv.at[5])])

    def pack(place, value, packed):
        turned = pltpu.roll(value, place, 1) if place else value
        return jnp.where(lane16 == jnp.bitwise_and(edge + place, 127), turned, packed)

    @pl.loop(0, gy)
    def _(peer):
        message_copy(peer, gy).start()

    pl.when(lead_left)(lambda: start(left))
    pl.when(lead_right)(lambda: start(right))
    start(down)

    for copy in (loads[8], loads[9]):
        copy.wait()
    speed = jnp.zeros((1, 128), F32)
    for layer in range(spd.shape[1]):
        speed = jnp.where(dep[...] == layer, spd[0:1, layer : layer + 1], speed)
    rate[1:17, 16:32] = lat[1:17, 16:32] * speed[None]
    packed, packed_rate = jnp.zeros((16, 128), F32), jnp.zeros((16, 128), F32)
    for c in range(3):
        for x in range(16):
            packed = pack(16 * c + x, U[0, c, x + 2, 16:32], packed)
            packed_rate = pack(16 * c + x, rate[x + 1, 16:32], packed_rate)
    zsend[0] = packed
    zsend[1] = packed_rate
    pl.when(lead_z)(lambda: start(across))

    loads[3].wait()
    k48 = lax.broadcasted_iota(jnp.int32, (48, 384), 0)
    q48 = lax.broadcasted_iota(jnp.int32, (48, 384), 1)
    late = k48 >= 32
    slot = jnp.where(late, (k48 - 32) // 8, k48 // 16)
    src = jnp.where(late, 16 + k48 % 8, k48 % 16)
    mine = jnp.logical_and(own[...] == gy + 64 * slot, q48 // 16 == src)
    slot_block = jnp.sum(jnp.where(mine, blk[...] + 1, 0), axis=1, keepdims=True) - 1
    column = lax.shift_right_arithmetic(slot_block, 3)
    hot = jnp.where(column == lax.broadcasted_iota(jnp.int32, (48, 256), 1), 1.0, 0.0)
    hot = jnp.transpose(jnp.concatenate([hot, jnp.zeros((80, 256), F32)], axis=0)).astype(BF16)
    hot_early = jnp.concatenate([hot[:, :32], hot[:, :32]], axis=1)
    hot_late = jnp.concatenate([hot[:, 32:48], hot[:, 32:48]], axis=1)

    loads[6].wait()

    def turned_rows(first, count, at):
        out = []
        for s in range(2):
            zb = jnp.bitwise_and(slot_block[at + count * s : at + count * (s + 1)], 7)
            for c in range(3):
                row = mrecv[first : first + count, c, :]
                for b in range(3):
                    row = jnp.where(jnp.bitwise_and(zb, 1 << b) > 0, pltpu.roll(row, 16 << b, 1), row)
                out.append((s, c, zb, row))
        return out

    def placed(rows, count, hot, *steps):
        lanes = lax.broadcasted_iota(jnp.int32, (count, 128), 1) // 16
        parts = [[], []]
        for n in steps:
            for s, c, zb, row in rows:
                shift = (-16 * (4 * s + n)) % 128
                moved = pltpu.roll(row, shift, 1) if shift else row
                parts[s].append(jnp.where(lanes == zb, moved, 0.0))
        w = jnp.concatenate([jnp.concatenate(part, axis=1) for part in parts], axis=0)
        return jnp.dot(hot, two_parts(w), preferred_element_type=F32)

    def stencil(step, c, x, halo, lo=16, rows=16):
        here = pl.ds(lo, rows)
        v = U[step, c, x + 2, here]
        lanes = lax.broadcasted_iota(jnp.int32, (rows, 128), 1)
        z = (
            jnp.where(lanes == 0, 0.0, pltpu.roll(v, 1, 1))
            + jnp.where(lanes == 127, 0.0, pltpu.roll(v, 127, 1))
            + jnp.where(lanes == edge, halo, 0.0)
        )
        y = U[step, c, x + 2, pl.ds(lo - 1, rows)] + U[step, c, x + 2, pl.ds(lo + 1, rows)]
        around = (U[step, c, x + 1, here] + U[step, c, x + 3, here]) + y + z
        old = up[c, x] if step == 0 else U[step - 1, c, x + 2, here]
        return (2.0 * v - old) + rate[x + 1, here] * (around - 6.0 * v)

    def to_edge(packed, place):
        return pltpu.roll(packed, 128 - place, 1) if place else packed

    order = [0, 15, 1, 14] + list(range(2, 14))

    def received(packed):
        return pltpu.roll(packed, jnp.bitwise_and(127 + 2 * gz, 127), 1)

    def answer(came, reply):
        arrive(came)
        start(reply)

    pl.when(jnp.logical_not(lead_z))(lambda: answer(across, across))
    answer(down, up_gy)
    pl.when(jnp.logical_not(lead_right))(lambda: answer(left, right))
    pl.when(gx == middle)(lambda: answer(right, left))

    def message_wait(peer):
        message_copy(peer, peer).wait_recv()

    def message_reply(peer):
        message_copy(peer, peer).wait_recv()
        message_copy(peer, gy).start()

    answered = jnp.where(jnp.logical_and(gx == 0, gy == 0), 6, gy + 1)
    pl.loop(gy + 1, answered)(message_reply)
    pl.when(lead_z)(lambda: arrive(across))
    arrive(up_gy)
    pl.when(lead_right)(lambda: arrive(left))
    pl.when(gx != middle)(lambda: arrive(right))
    sides = [(-1, 0, 0), (1, 0, 0), (0, -1, 0), (0, 1, 0)]
    beside_count = 0
    for to in sides:
        there = exists(to[0], to[1])
        beside_count = beside_count + there.astype(jnp.int32)
        pl.when(there)(
            lambda to=to: pl.semaphore_signal(known, inc=1, device_id=device(*to), device_id_type=MESH)
        )
    rate[0:1, 16:32] = lat[0:1, 16:32] * speed[None]
    rate[17:18, 16:32] = lat[17:18, 16:32] * speed[None]
    rate[1:17, 8:16] = lat[1:17, 8:16] * speed[None]
    rate[1:17, 32:40] = lat[1:17, 32:40] * speed[None]
    halo0 = received(zrecv[0])
    for x in order:
        for c in range(3):
            U[1, c, x + 2, 16:32] = stencil(0, c, x, to_edge(halo0, 16 * c + x))

    turn = jnp.where(gy < 8, 16, n_gy)
    pl.loop(answered, turn)(message_reply)
    pl.loop(0, jnp.minimum(gy, 16))(message_wait)
    rows = turned_rows(0, 16, 0)
    D[0] = placed(rows, 16, hot_early, 0)
    D1[:, 16:32] = placed(rows, 16, hot_early, 1).reshape(16, 16, 384)
    for n in (2, 3):
        D[n - 1] = placed(rows, 16, hot_early, n)
    pl.loop(turn, n_gy)(message_reply)
    pl.loop(16, gy)(message_wait)
    rows = turned_rows(16, 8, 32)
    both = placed(rows, 8, hot_late, 0, 1)
    drive = D[0] + both[:, :384]
    D1[:, 16:32] = D1[:, 16:32] + both[:, 384:].reshape(16, 16, 384)
    edge_1 = inner_1 = edge_d = jnp.zeros((16, 128), F32)
    inward = jnp.where(gz == 0, 1, 127)
    for x in order:
        for c in range(3):
            new = U[1, c, x + 2, 16:32] + drive[16 * x : 16 * x + 16, 128 * c : 128 * c + 128]
            U[1, c, x + 2, 16:32] = new
            edge_1 = pack(16 * c + x, new, edge_1)
            inner_1 = pack(16 * c + x, pltpu.roll(new, inward, 1), inner_1)
            edge_d = pack(16 * c + x, D1[x, 16:32, 128 * c : 128 * c + 128], edge_d)
        if x == 14:
            start(deep_x)
    zsend[2] = edge_1
    zsend[3] = inner_1
    zsend[4] = edge_d
    pl.semaphore_wait(known, beside_count)
    start(corners)
    start(deep_xz)
    start(deep_y)
    start(deep_z)
    for n in (2, 3):
        D[n - 1] = D[n - 1] + placed(rows, 8, hot_late, n)

    arrive(deep_z)
    arrive(deep_y)
    halo1 = received(zrecv[2])
    tall = received(jnp.concatenate([zrow[0], zrecv[2], zrow[1]], axis=0))[4:28]

    def second(x):
        for c in range(3):
            U[2, c, x + 2, 12:36] = (
                stencil(1, c, x, to_edge(tall, 16 * c + x), 12, 24) + D1[x, 12:36, 128 * c : 128 * c + 128]
            )

    for x in range(1, 15):
        second(x)
    arrive(corners)
    arrive(deep_xz)
    arrive(deep_x)
    left1, right1 = received(zside[0]), received(zside[1])
    for c in range(3):
        U[2, c, 1, 16:32] = stencil(1, c, -1, to_edge(left1, 16 * c + 15)) + D1x[0, :, 128 * c : 128 * c + 128]
        U[2, c, 18, 16:32] = stencil(1, c, 16, to_edge(right1, 16 * c)) + D1x[1, :, 128 * c : 128 * c + 128]
    second(0)
    second(15)
    x_of = jnp.bitwise_and(lane16 - edge, 15)
    beside = (
        jnp.where(x_of == 0, pltpu.roll(left1, 113, 1), pltpu.roll(halo1, 1, 1))
        + jnp.where(x_of == 15, pltpu.roll(right1, 15, 1), pltpu.roll(halo1, 127, 1))
        + tall[3:19] + tall[5:21] + edge_1 + received(zrecv[3])
    )
    halo = (2.0 * halo1 - halo0) + received(zrecv[1]) * (beside - 6.0 * halo1) + received(zrecv[4])

    packed = jnp.zeros((16, 128), F32)
    for x in order:
        for c in range(3):
            drive = D[1, 16 * x : 16 * x + 16, 128 * c : 128 * c + 128]
            new = stencil(2, c, x, to_edge(halo, 16 * c + x)) + drive
            U[3, c, x + 2, 16:32] = new
            packed = pack(16 * c + x, new, packed)
            out_prev[c, x] = new
        if x == 15:
            start(last_x)
    zsend[5] = packed
    start(last_yz)

    arrive(last_yz)
    halo = received(zrecv[5])

    def last(x):
        for c in range(3):
            drive = D[2, 16 * x : 16 * x + 16, 128 * c : 128 * c + 128]
            out_now[c, x] = stencil(3, c, x, to_edge(halo, 16 * c + x)) + drive

    for x in range(1, 15):
        last(x)
    arrive(last_x)
    last(0)
    last(15)

    for copies in (left, right, down, up_gy, across, deep_x, corners, deep_y, deep_xz, deep_z, last_x, last_yz):
        sent(copies)

    @pl.loop(1, n_gy)
    def _(k):
        message_copy(lax.rem(gy + k, n_gy), gy).wait_send()


def write_out(now_in, prev_in, now_out, prev_out, sem):
    copies = [pltpu.make_async_copy(now_in, now_out, sem.at[0]), pltpu.make_async_copy(prev_in, prev_out, sem.at[1])]
    for copy in copies:
        copy.start()
    for copy in copies:
        copy.wait()


def per_device(n_gx, n_gy, u_now, u_prev, panels, panel_owner, panel_block, coupling, layer_depth, layer_speed, lateral):
    spectral = panels.shape[4]
    count = panel_owner.shape[2]
    layers = layer_speed.shape[0]
    table = jnp.asarray(wave_table(spectral))
    anywhere = pl.BlockSpec(memory_space=pl.ANY)
    vmem = pl.BlockSpec(memory_space=pltpu.VMEM)
    dma = pltpu.SemaphoreType.DMA
    now, prev = pl.pallas_call(
        functools.partial(kernel, n_gx, n_gy),
        out_shape=(pltpu.VMEM(u_now.shape, F32), pltpu.VMEM(u_now.shape, F32)),
        in_specs=[anywhere] * 10,
        out_specs=(vmem, vmem),
        scratch_shapes=[
            pltpu.VMEM((NSTEP, 3, 20, 48, 128), F32),
            pltpu.VMEM(u_prev.shape, F32),
            pltpu.VMEM((768, spectral), BF16),
            pltpu.VMEM((1, count), jnp.int32),
            pltpu.VMEM((1, count), jnp.int32),
            pltpu.VMEM(coupling.shape, F32),
            pltpu.VMEM((1, 128), jnp.int32),
            pltpu.VMEM((1, layers), F32),
            pltpu.VMEM((18, 48, 128), F32),
            pltpu.VMEM(table.shape, BF16),
            pltpu.VMEM((8, 16, 128), F32),
            pltpu.VMEM((3, 256, 384), F32),
            pltpu.VMEM((24, 3, 128), F32),
            pltpu.VMEM((24, 3, 128), F32),
            pltpu.VMEM((18, 48, 128), F32),
            pltpu.VMEM((16, 48, 384), F32),
            pltpu.VMEM((2, 16, 384), F32),
            pltpu.VMEM((6, 16, 128), F32),
            pltpu.VMEM((6, 16, 128), F32),
            pltpu.VMEM((2, 16, 128), F32),
            pltpu.VMEM((2, 8, 128), F32),
            dma((10,)),
            dma((24,)),
            dma((24,)),
            dma((31,)),
            dma((31,)),
            pltpu.SemaphoreType.REGULAR,
        ],
        compiler_params=pltpu.CompilerParams(collective_id=0, has_side_effects=True),
        name="domain_reduction",
    )(
        u_now, u_prev, panels.reshape(768, spectral), panel_owner.reshape(1, count), panel_block.reshape(1, count),
        coupling, layer_depth.reshape(1, 128), layer_speed.reshape(1, layers), lateral, table,
    )
    whole = jax.ShapeDtypeStruct(u_now.shape, F32)
    return pl.pallas_call(
        write_out,
        out_shape=(whole, whole),
        in_specs=[vmem, vmem],
        out_specs=(anywhere, anywhere),
        scratch_shapes=[dma((2,))],
        name="write_out",
    )(
        pltpu.with_memory_space_constraint(now, pltpu.VMEM),
        pltpu.with_memory_space_constraint(prev, pltpu.VMEM),
    )


def solution(mesh):
    in_specs = (
        P(None, "gx", "gy", "gz"),
        P(None, "gx", "gy", "gz"),
        P("gx", "gz", "gy", None, None),
        P("gx", "gz", None, None),
        P("gx", "gz", None),
        P(),
        P("gz"),
        P(),
        P("gx", "gy", "gz"),
    )
    out_specs = (P(None, "gx", "gy", "gz"), P(None, "gx", "gy", "gz"))
    return jax.shard_map(
        functools.partial(per_device, mesh.shape["gx"], mesh.shape["gy"]),
        mesh=mesh, in_specs=in_specs, out_specs=out_specs, check_vma=False,
    )
```
